512 devices in a mesh: head: 8 (over z), tok: 64 (over x, y, core).
Axes of the slice: x: 4, y: 8, z: 8, core: 2. Of those that a mesh axis runs over, the one named last changes fastest.
Arguments:
- patches: bfloat16 [32768, 1280], P('tok')
- row_table: bfloat16 [64, 1280], replicated, may hold values from -0.59765625 to 0.59765625
- col_table: bfloat16 [64, 1280], replicated, may hold values from -0.59765625 to 0.59765625
- qkv_weight: bfloat16 [3, 1280, 1280], P(None, 'head'), may hold values from -0.15625 to 0.15625
- out_weight: bfloat16 [1280, 1280], P('head'), may hold values from -0.15625 to 0.15625
- merge_weight: bfloat16 [1280, 5120], P('head'), may hold values from -0.078125 to 0.078125
- segment_ids: int32 [32768], P('tok'), may hold values from 0 to 63, as said below
- image_grids: int32 [64, 2], replicated, may hold values from 2 to 62, as said below
- image_offsets: int32 [64], replicated, may hold values from 0 to 32736, as said below
- owners: int32 [64], replicated, may hold values from 0 to 63, each once
Outputs:
- delivered: bfloat16 [15872, 1280], P('tok', 'head')
The draws below stay inside these ranges and needn't reach their ends.
Inputs may be any that keep to these rules, and one draw needn't show every extreme that they name: `segment_ids`: tokens of each image are consecutive and images follow in order; the pair p of token blocks (tokens 2 * p * 512 to 2 * (p + 1) * 512 - 1) holds exactly images 2 * p and 2 * p + 1, with no padding. `image_grids`: heights are even, widths are 16, and height times width is the image's token count. Within an image each 2x2 window of patches is four consecutive tokens (top left, top right, bottom left, bottom right), windows in row-major order. The longest image has exactly 992 tokens. `image_offsets`: the first token of each image, consistent with segment_ids. `owners`: every device index along tok owns exactly one image.
All inputs are finite; a program needn't handle non-finite values.
Results may differ from the reference program's by a relative error of at most 0.019.
Values may be sent and summed in bfloat16 or wider, within the bound.
No kernel may reach another device: no remote copies, remote signals or barrier semaphores. Data moves between devices by JAX's collectives and lax.ppermute only.
A program may use at most 64 MiB of HBM per device.

```python
import math
import jax
import jax.numpy as jnp
from jax import lax

D = 1280
HEADS = 16
HEAD_DIM = 80
MAXSIDE = 64
TOK_BLK = 512
TOKENS = 32768
IMAGES = 64
CAP = 248
N_TOK = 64


def pair_layout(key):
    base_key = jax.random.fold_in(key, 7)
    key_height = jax.random.fold_in(base_key, 1)
    key_forced = jax.random.fold_in(base_key, 2)
    pair_count = IMAGES // 2
    forced_pair = jax.random.randint(key_forced, (), 0, pair_count)
    is_forced = jnp.arange(pair_count) == forced_pair
    width_pair = jnp.full((pair_count,), 16, jnp.int32)
    total_rows = 2 * TOK_BLK // width_pair
    middle_rows = TOK_BLK // 16
    choice_count = total_rows // 2 - 2
    height_draw = jax.random.randint(key_height, (pair_count,), 0, 1000000)
    height_first = 2 * (1 + height_draw % choice_count)
    height_first = jnp.where(height_first >= middle_rows, height_first + 2, height_first)
    height_first = jnp.where(is_forced, total_rows - 2, height_first)
    length_first = height_first * width_pair
    return (width_pair, total_rows, height_first, length_first)


def draw_segment_ids(key, part):
    width_pair, total_rows, height_first, length_first = pair_layout(key)
    token_pos = jnp.arange(TOKENS, dtype=jnp.int32)
    pair_index = token_pos // (2 * TOK_BLK)
    local_pos = token_pos % (2 * TOK_BLK)
    second_flag = (local_pos >= length_first[pair_index]).astype(jnp.int32)
    return (2 * pair_index + second_flag).astype(jnp.int32)


def draw_image_grids(key, part):
    width_pair, total_rows, height_first, length_first = pair_layout(key)
    heights = jnp.stack([height_first, total_rows - height_first], axis=1).reshape(IMAGES)
    widths = jnp.stack([width_pair, width_pair], axis=1).reshape(IMAGES)
    return jnp.stack([heights, widths], axis=1).astype(jnp.int32)


def draw_image_offsets(key, part):
    width_pair, total_rows, height_first, length_first = pair_layout(key)
    pair_start = 2 * TOK_BLK * jnp.arange(IMAGES // 2, dtype=jnp.int32)
    return jnp.stack([pair_start, pair_start + length_first], axis=1).reshape(IMAGES).astype(jnp.int32)


def draw_patches(key, part):
    key_rows, key_cols, key_base = jax.random.split(key, 3)
    row_scale = jnp.exp(jax.random.uniform(key_rows, (TOKENS, 1), jnp.float32, math.log(0.03), math.log(0.3)))
    col_scale = jnp.exp(jax.random.uniform(key_cols, (1, D), jnp.float32, math.log(0.5), math.log(5.0)))
    base_values = jax.random.normal(key_base, (TOKENS, D), jnp.float32)
    return (base_values * row_scale * col_scale).astype(jnp.bfloat16)


def shard_levels(rng, shape, shards, least, largest):
    gain, own = 1.0, jax.random.fold_in(rng, 6)
    for position, blocks in shards:
        steps = jnp.exp(jax.random.uniform(jax.random.fold_in(own, position), (blocks,), jnp.float32, least / len(shards), largest / len(shards)))
        gain = gain * jnp.repeat(steps, shape[position] // blocks).reshape([-1 if axis == position else 1 for axis in range(len(shape))])
    return gain


def normal_values(rng, shape, scale, bound, pieces=(), kind=jnp.bfloat16):
    result = jax.random.normal(rng, shape, jnp.float32) * scale
    if len(pieces) > 0:
        result = shard_levels(rng, shape, pieces, -0.22, 0.18) * result
    return jnp.clip(result, min=-bound, max=bound).astype(kind)


def setup_inputs(seed: int = 0) -> dict:
    seeds = jax.random.split(jax.random.key(seed), 11)
    return {
        "patches": draw_patches(jax.random.fold_in(seeds[10], 71), 0),
        "row_table": normal_values(seeds[1], (MAXSIDE, D), 0.1, 0.59765625),
        "col_table": normal_values(seeds[2], (MAXSIDE, D), 0.1, 0.59765625),
        "qkv_weight": normal_values(seeds[3], (3, D, D), D ** -0.5, 0.15625, ((1, 8),)),
        "out_weight": normal_values(seeds[4], (D, D), D ** -0.5, 0.15625, ((0, 8),)),
        "merge_weight": normal_values(seeds[5], (D, 4 * D), (4 * D) ** -0.5, 0.078125, ((0, 8),)),
        "segment_ids": draw_segment_ids(jax.random.fold_in(seeds[10], 71), 0),
        "image_grids": draw_image_grids(jax.random.fold_in(seeds[10], 71), 0),
        "image_offsets": draw_image_offsets(jax.random.fold_in(seeds[10], 71), 0),
        "owners": jax.random.permutation(seeds[9], N_TOK).astype(jnp.int32),
    }


def layer_norm(values):
    centered = values - lax.optimization_barrier(jnp.mean(values, axis=-1, keepdims=True))
    variance = lax.optimization_barrier(jnp.mean(centered * centered, axis=-1, keepdims=True))
    return centered * lax.rsqrt(variance + 1e-06)

def grid_place(token_pos, start_tok, width_now):
    local_pos = token_pos - start_tok
    window = local_pos // 4
    quarter = local_pos % 4
    half_width = jnp.maximum(width_now // 2, 1)
    row_index = 2 * (window // half_width) + quarter // 2
    col_index = 2 * (window % half_width) + quarter % 2
    return (row_index.astype(jnp.int32), col_index.astype(jnp.int32))

def reference(patches, row_table, col_table, qkv_weight, out_weight, merge_weight, segment_ids, image_grids, image_offsets, owners):
    token_pos = jnp.arange(TOKENS, dtype=jnp.int32)
    row_index, col_index = grid_place(token_pos, image_offsets[segment_ids], image_grids[segment_ids, 1])
    resid = patches.astype(jnp.float32) + row_table[row_index].astype(jnp.float32) + col_table[col_index].astype(jnp.float32)
    normed = layer_norm(resid).astype(jnp.bfloat16)
    queries = jnp.dot(normed, qkv_weight[0].T, preferred_element_type=jnp.float32).astype(jnp.bfloat16)
    key_rows = jnp.dot(normed, qkv_weight[1].T, preferred_element_type=jnp.float32).astype(jnp.bfloat16)
    value_rows = jnp.dot(normed, qkv_weight[2].T, preferred_element_type=jnp.float32).astype(jnp.bfloat16)
    span = 2 * TOK_BLK
    pair_count = TOKENS // span
    scale_factor = 1.0 / math.sqrt(HEAD_DIM)

    def attend_pair(inputs):
        query_part, key_part, value_part, seg_part = inputs
        query_heads = query_part.reshape(span, HEADS, HEAD_DIM).astype(jnp.float32)
        key_heads = key_part.reshape(span, HEADS, HEAD_DIM).astype(jnp.float32)
        value_heads = value_part.reshape(span, HEADS, HEAD_DIM).astype(jnp.float32)
        scores = jnp.einsum('qhd,khd->hqk', query_heads, key_heads) * scale_factor
        same_image = seg_part[:, None] == seg_part[None, :]
        raw_weights = jnp.where(same_image[None], jnp.exp(scores), 0.0)
        weight_sum = lax.optimization_barrier(jnp.sum(raw_weights, axis=-1, keepdims=True))
        attn_probs = (raw_weights / weight_sum).astype(jnp.bfloat16)
        mixed = jnp.einsum('hqk,khd->qhd', attn_probs.astype(jnp.float32), value_heads)
        return mixed.reshape(span, D).astype(jnp.bfloat16)
    attended = lax.map(attend_pair, (queries.reshape(pair_count, span, D), key_rows.reshape(pair_count, span, D), value_rows.reshape(pair_count, span, D), segment_ids.reshape(pair_count, span)))
    attended = attended.reshape(TOKENS, D)
    resid_two = resid + jnp.dot(attended, out_weight, preferred_element_type=jnp.float32)
    normed_two = layer_norm(resid_two).astype(jnp.bfloat16)
    merged = normed_two.reshape(TOKENS // 4, 4 * D)
    projected = jnp.dot(merged, merge_weight.T, preferred_element_type=jnp.float32).astype(jnp.bfloat16)
    padded = jnp.concatenate([projected, jnp.zeros((CAP, D), projected.dtype)], axis=0)
    image_ids = jnp.arange(IMAGES, dtype=jnp.int32)

    def deliver(owner_id):
        image_id = jnp.sum(jnp.where(owners == owner_id, image_ids, 0)).astype(jnp.int32)
        first_row = (image_offsets[image_id] // 4).astype(jnp.int32)
        merged_count = image_grids[image_id, 0] * image_grids[image_id, 1] // 4
        rows_here = lax.dynamic_slice_in_dim(padded, first_row, CAP, 0)
        keep_rows = jnp.arange(CAP, dtype=jnp.int32) < merged_count
        return jnp.where(keep_rows[:, None], rows_here, jnp.zeros_like(rows_here))
    delivered = lax.map(deliver, jnp.arange(N_TOK, dtype=jnp.int32))
    return delivered.reshape(N_TOK * CAP, D)
```

```python
import math

import jax
import jax.numpy as jnp
from jax import lax
from jax.sharding import PartitionSpec as P

HEAD_DIM = 80
CAP = 248


def partner(x, axis, apart):
    return lax.ppermute(x, axis, [(i, i ^ 1 << apart) for i in range(lax.axis_size(axis))])


def layer_norm(values):
    centered = values - jnp.mean(values, axis=-1, keepdims=True)
    variance = jnp.mean(centered * centered, axis=-1, keepdims=True)
    return centered * lax.rsqrt(variance + 1e-06)


def grid_place(token_pos, start_tok, width_now):
    local_pos = token_pos - start_tok
    window = local_pos // 4
    quarter = local_pos % 4
    half_width = jnp.maximum(width_now // 2, 1)
    row_index = 2 * (window // half_width) + quarter // 2
    col_index = 2 * (window % half_width) + quarter % 2
    return (row_index, col_index)


def dot_last(left, right):
    return lax.dot_general(
        left, right, (((1,), (1,)), ((), ())), preferred_element_type=jnp.float32
    )


def on_device(
    patches,
    row_table,
    col_table,
    qkv_weight,
    out_weight,
    merge_weight,
    segment_ids,
    image_grids,
    image_offsets,
    owners,
):
    full_weight = lax.all_gather(out_weight, "head", axis=0, tiled=True)
    block_rows = patches.shape[0]
    width_here = qkv_weight.shape[1]
    heads_here = width_here // HEAD_DIM
    image_count = owners.shape[0]
    image_ids = jnp.arange(image_count, dtype=jnp.int32)
    token_pos = lax.axis_index("tok") * block_rows + jnp.arange(block_rows, dtype=jnp.int32)
    member = segment_ids[:, None] == image_ids[None, :]
    start_tok = jnp.sum(jnp.where(member, image_offsets[None, :], 0), axis=1)
    width_now = jnp.sum(jnp.where(member, image_grids[None, :, 1], 0), axis=1)
    row_index, col_index = grid_place(token_pos, start_tok, width_now)
    side_ids = jnp.arange(row_table.shape[0], dtype=jnp.int32)
    row_onehot = (row_index[:, None] == side_ids[None, :]).astype(jnp.bfloat16)
    col_onehot = (col_index[:, None] == side_ids[None, :]).astype(jnp.bfloat16)
    resid = (
        patches.astype(jnp.float32)
        + jnp.dot(row_onehot, row_table, preferred_element_type=jnp.float32)
        + jnp.dot(col_onehot, col_table, preferred_element_type=jnp.float32)
    )
    normed = layer_norm(resid).astype(jnp.bfloat16)
    query_rows = dot_last(normed, qkv_weight[0]).astype(jnp.bfloat16)
    key_rows = dot_last(normed, qkv_weight[1]).astype(jnp.bfloat16)
    value_rows = dot_last(normed, qkv_weight[2]).astype(jnp.bfloat16)
    seg_wire = segment_ids.astype(jnp.bfloat16)
    far_keys, far_values, far_seg = partner((key_rows, value_rows, seg_wire), "tok", 0)
    query_heads = query_rows.reshape(block_rows, heads_here, HEAD_DIM)
    key_heads = jnp.concatenate([key_rows, far_keys], axis=0).reshape(
        2 * block_rows, heads_here, HEAD_DIM
    )
    value_heads = jnp.concatenate([value_rows, far_values], axis=0).reshape(
        2 * block_rows, heads_here, HEAD_DIM
    )
    query_seg = seg_wire.astype(jnp.float32)
    key_seg = jnp.concatenate([seg_wire, far_seg], axis=0).astype(jnp.float32)
    scores = jnp.einsum(
        "qhd,khd->hqk", query_heads, key_heads, preferred_element_type=jnp.float32
    ) * (1.0 / math.sqrt(HEAD_DIM))
    same_image = query_seg[:, None] == key_seg[None, :]
    raw_weights = jnp.where(same_image[None], jnp.exp(scores), 0.0)
    weight_sum = jnp.sum(raw_weights, axis=-1, keepdims=True)
    attn_probs = (raw_weights / weight_sum).astype(jnp.bfloat16)
    mixed = jnp.einsum("hqk,khd->qhd", attn_probs, value_heads, preferred_element_type=jnp.float32)
    attended = mixed.reshape(block_rows, width_here).astype(jnp.bfloat16)
    group = lax.axis_size("head")
    sent = jnp.broadcast_to(attended[None], (group,) + attended.shape)
    gathered = lax.all_to_all(sent, "head", 0, 0, tiled=True)
    head_total = jnp.einsum(
        "ztf,zfd->td",
        gathered,
        full_weight.reshape(group, width_here, -1),
        preferred_element_type=jnp.float32,
    )
    normed_two = layer_norm(resid + head_total).astype(jnp.bfloat16)
    merged = normed_two.reshape(block_rows // 4, 4 * normed_two.shape[1])
    projected = dot_last(merged, merge_weight).astype(jnp.bfloat16)

    places = lax.axis_size("tok")
    rows_here = projected.shape[0]
    share = rows_here // places
    spread = lax.all_to_all(projected.reshape(places, share, width_here), "tok", 0, 0, tiled=True)
    pair_ids = jnp.arange(places // 2, dtype=jnp.int32)
    place_ids = jnp.arange(places, dtype=jnp.int32)
    wanted = (owners.reshape(-1, 2)[None, :, :] == place_ids[:, None, None]).any(axis=2)
    pieces = jnp.dot(
        wanted.astype(jnp.bfloat16),
        spread.reshape(places // 2, 2 * share * width_here),
        preferred_element_type=jnp.float32,
    ).astype(jnp.bfloat16)
    pair_rows = lax.all_to_all(
        pieces.reshape(places, 2 * share, width_here), "tok", 0, 0, tiled=True
    ).reshape(2 * rows_here, width_here)

    owner_mask = owners == lax.axis_index("tok")
    image_id = jnp.sum(jnp.where(owner_mask, image_ids, 0))
    first_row = jnp.sum(jnp.where(owner_mask, image_offsets, 0)) // 4 - (image_id // 2) * 2 * rows_here
    merged_count = jnp.sum(jnp.where(owner_mask, image_grids[:, 0] * image_grids[:, 1], 0)) // 4
    slot_ids = jnp.arange(CAP, dtype=jnp.int32)
    got_ids = jnp.arange(2 * rows_here, dtype=jnp.int32)
    row_of = (got_ids // share % 2) * rows_here + got_ids // (2 * share) * share + got_ids % share
    slot_of = row_of - first_row
    selector = (slot_of[None, :] == slot_ids[:, None]) & (slot_ids < merged_count)[:, None]
    owner_rows = jnp.dot(
        selector.astype(jnp.bfloat16), pair_rows, preferred_element_type=jnp.float32
    )
    return owner_rows.astype(jnp.bfloat16)


def solution(mesh):
    placed = (
        P("tok", None),
        P(),
        P(),
        P(None, "head", None),
        P("head", None),
        P("head", None),
        P("tok"),
        P(),
        P(),
        P(),
    )
    return jax.shard_map(
        on_device, mesh=mesh, in_specs=placed, out_specs=P("tok", "head"), check_vma=False
    )
```

```python
import math

import jax
import jax.numpy as jnp
from jax import lax
from jax.experimental import pallas as pl
from jax.experimental.pallas import tpu as pltpu
from jax.sharding import PartitionSpec as P

HEAD_DIM = 80
CAP = 248
WIDTH = 16
LANES = 128
SCALE = 1.0 / math.sqrt(HEAD_DIM)
MASKED = -1e30

VMEM = pl.BlockSpec(memory_space=pltpu.VMEM)
SMEM = pl.BlockSpec(memory_space=pltpu.SMEM)


def partner(x, axis, apart):
    return lax.ppermute(x, axis, [(i, i ^ 1 << apart) for i in range(lax.axis_size(axis))])


def normalize(values):
    centered = values - jnp.mean(values, axis=-1, keepdims=True)
    variance = jnp.mean(centered * centered, axis=-1, keepdims=True)
    return centered * lax.rsqrt(variance + 1e-06)


def dot(left, right, dims):
    return lax.dot_general(left, right, (dims, ((), ())), preferred_element_type=jnp.float32)


def front_kernel(offsets, patches, row_table, col_table, weight, resid, queries, pairs):
    rows = patches.shape[0]
    side = row_table.shape[0]
    place = lax.axis_index("tok")
    first = place // 2 * 2
    position = place * rows + lax.broadcasted_iota(jnp.int32, (rows, 2 * side), 0)
    start = jnp.where(position >= offsets[first + 1], offsets[first + 1], offsets[first])
    local = position - start
    window = local >> 2
    quarter = local & 3
    half = WIDTH // 2
    row = 2 * (window // half) + (quarter >> 1)
    col = 2 * (window % half) + (quarter & 1)
    lane = lax.broadcasted_iota(jnp.int32, (rows, 2 * side), 1)
    onehot = lane == jnp.where(lane < side, row, col + side)
    tables = jnp.concatenate([row_table[...], col_table[...]], axis=0)
    onehot = jnp.where(onehot, 1.0, 0.0).astype(jnp.bfloat16)
    values = patches[...].astype(jnp.float32) + dot(onehot, tables, ((1,), (0,)))
    resid[...] = values
    normed = normalize(values).astype(jnp.bfloat16)
    width = weight.shape[1]
    wide = weight[...].reshape(3 * width, weight.shape[2])
    out = dot(wide, normed, ((1,), (1,))).astype(jnp.bfloat16)
    queries[...] = out[:width]
    pairs[...] = out[width:]


def attend_kernel(offsets, queries, near, far, out):
    rows = queries.shape[1]
    width = queries.shape[0]
    place = lax.axis_index("tok")
    core = place % 2
    border = offsets[place // 2 * 2 + 1]
    ahead = jnp.where(core == 0, rows, -rows)
    query_pos = place * rows + lax.broadcasted_iota(jnp.int32, (1, rows), 1)
    key_pos = place * rows + lax.broadcasted_iota(jnp.int32, (rows, 1), 0)
    query_side = jnp.where(query_pos >= border, 1, 0)
    near_side = jnp.where(key_pos >= border, 1, 0)
    far_side = jnp.where(key_pos + ahead >= border, 1, 0)
    for head in range(width // HEAD_DIM):
        own = slice(head * HEAD_DIM, (head + 1) * HEAD_DIM)
        value = slice(width + head * HEAD_DIM, width + (head + 1) * HEAD_DIM)
        query = queries[own, :]
        near_scores = dot(near[own, :], query, ((0,), (0,)))
        far_scores = dot(far[own, :], query, ((0,), (0,)))
        near_scores = jnp.where(near_side == query_side, near_scores * SCALE, MASKED)
        far_scores = jnp.where(far_side == query_side, far_scores * SCALE, MASKED)
        top = jnp.maximum(
            jnp.max(near_scores, axis=0, keepdims=True), jnp.max(far_scores, axis=0, keepdims=True)
        )
        near_expo = jnp.exp(near_scores - top)
        far_expo = jnp.exp(far_scores - top)
        total = jnp.sum(near_expo, axis=0, keepdims=True) + jnp.sum(far_expo, axis=0, keepdims=True)
        mixed = dot(near[value, :], near_expo.astype(jnp.bfloat16), ((1,), (0,)))
        mixed += dot(far[value, :], far_expo.astype(jnp.bfloat16), ((1,), (0,)))
        mixed = (mixed / total).astype(jnp.bfloat16)
        slot = pl.multiple_of(jnp.where(core == head, 0, HEAD_DIM), 16)
        for copy in range(out.shape[0]):
            out[copy, pl.ds(slot, HEAD_DIM), :] = mixed


def merge_kernel(gathered, own_weight, other_weight, resid, merge_weight, out, attended, normed):
    group = gathered.shape[0]
    depth = group * HEAD_DIM
    for head in range(2):
        for place in range(group):
            attended[pl.ds(head * depth + place * HEAD_DIM, HEAD_DIM), :] = gathered[
                place, head * HEAD_DIM : (head + 1) * HEAD_DIM, :
            ]
    total = resid[...] + dot(attended[:depth, :], own_weight[...], ((0,), (0,)))
    total += dot(attended[depth:, :], other_weight[...], ((0,), (0,)))
    rows, width = total.shape
    total = normalize(total)
    for tile in range(width // LANES):
        normed[tile] = total[:, tile * LANES : (tile + 1) * LANES]
    projected = jnp.zeros(out.shape, jnp.float32)
    for quarter in range(4):
        part = [
            normed[tile, pl.ds(quarter, rows // 4, stride=4), :] for tile in range(width // LANES)
        ]
        part = jnp.concatenate(part, axis=1).astype(jnp.bfloat16)
        weight = merge_weight[:, quarter * width : (quarter + 1) * width]
        projected += dot(part, weight, ((1,), (1,)))
    out[...] = projected.astype(out.dtype)


def on_device(
    patches,
    row_table,
    col_table,
    qkv_weight,
    out_weight,
    merge_weight,
    segment_ids,
    image_grids,
    image_offsets,
    owners,
):
    block_rows, width = patches.shape
    width_here = qkv_weight.shape[1]
    group = lax.axis_size("head")
    places = lax.axis_size("tok")
    place = lax.axis_index("tok")
    params = pltpu.CompilerParams(vmem_limit_bytes=50 * 2**20)

    half_weight = lax.dynamic_slice_in_dim(out_weight, place % 2 * HEAD_DIM, HEAD_DIM, 0)
    own_weight = lax.all_gather(half_weight, "head", axis=0, tiled=True)
    other_weight = partner(own_weight, "tok", 0)

    resid, queries, near = pl.pallas_call(
        front_kernel,
        out_shape=(
            jax.ShapeDtypeStruct((block_rows, width), jnp.float32),
            jax.ShapeDtypeStruct((width_here, block_rows), jnp.bfloat16),
            jax.ShapeDtypeStruct((2 * width_here, block_rows), jnp.bfloat16),
        ),
        in_specs=[SMEM, VMEM, VMEM, VMEM, VMEM],
        out_specs=(VMEM, VMEM, VMEM),
        compiler_params=params,
    )(image_offsets, patches, row_table, col_table, qkv_weight)
    far = partner(near, "tok", 0)
    sent = pl.pallas_call(
        attend_kernel,
        out_shape=jax.ShapeDtypeStruct((group, width_here, block_rows), jnp.bfloat16),
        in_specs=[SMEM, VMEM, VMEM, VMEM],
        out_specs=VMEM,
        compiler_params=params,
    )(image_offsets, queries, near, far)
    gathered = lax.all_to_all(sent, "head", 0, 0, tiled=True)
    projected = pl.pallas_call(
        merge_kernel,
        out_shape=jax.ShapeDtypeStruct((block_rows // 4, width_here), jnp.bfloat16),
        in_specs=[VMEM, VMEM, VMEM, VMEM, VMEM],
        out_specs=VMEM,
        scratch_shapes=[
            pltpu.VMEM((group * width_here, block_rows), jnp.bfloat16),
            pltpu.VMEM((width // LANES, block_rows, LANES), jnp.float32),
        ],
        compiler_params=params,
    )(gathered, own_weight, other_weight, resid, merge_weight)

    rows_here = projected.shape[0]
    share = rows_here // places
    spread = lax.all_to_all(projected.reshape(places, share, width_here), "tok", 0, 0, tiled=True)
    place_ids = jnp.arange(places, dtype=jnp.int32)
    wanted = (owners.reshape(-1, 2)[None, :, :] == place_ids[:, None, None]).any(axis=2)
    pieces = jnp.dot(
        wanted.astype(jnp.bfloat16),
        spread.reshape(places // 2, 2 * share * width_here),
        preferred_element_type=jnp.float32,
    ).astype(jnp.bfloat16)
    pair_rows = lax.all_to_all(
        pieces.reshape(places, 2 * share, width_here), "tok", 0, 0, tiled=True
    ).reshape(2 * rows_here, width_here)

    image_ids = jnp.arange(owners.shape[0], dtype=jnp.int32)
    owner_mask = owners == place
    image_id = jnp.sum(jnp.where(owner_mask, image_ids, 0))
    first_row = jnp.sum(jnp.where(owner_mask, image_offsets, 0)) // 4
    first_row = first_row - (image_id // 2) * 2 * rows_here
    tokens = image_grids[:, 0] * image_grids[:, 1]
    merged_count = jnp.sum(jnp.where(owner_mask, tokens, 0)) // 4
    slot_ids = jnp.arange(CAP, dtype=jnp.int32)
    got_ids = jnp.arange(2 * rows_here, dtype=jnp.int32)
    row_of = (got_ids // share % 2) * rows_here + got_ids // (2 * share) * share + got_ids % share
    slot_of = row_of - first_row
    selector = (slot_of[None, :] == slot_ids[:, None]) & (slot_ids < merged_count)[:, None]
    owner_rows = jnp.dot(
        selector.astype(jnp.bfloat16), pair_rows, preferred_element_type=jnp.float32
    )
    return owner_rows.astype(jnp.bfloat16)


def solution(mesh):
    placed = (
        P("tok", None),
        P(),
        P(),
        P(None, "head", None),
        P("head", None),
        P("head", None),
        P("tok"),
        P(),
        P(),
        P(),
    )
    return jax.shard_map(
        on_device, mesh=mesh, in_specs=placed, out_specs=P("tok", "head"), check_vma=False
    )
```

```python
import math

import jax
import jax.numpy as jnp
from jax import lax
from jax.experimental import pallas as pl
from jax.experimental.pallas import tpu as pltpu
from jax.sharding import PartitionSpec as P

HEAD_DIM = 80
CAP = 248
WIDTH = 16
LANES = 128
RING = 8
SCALE = 1.0 / math.sqrt(HEAD_DIM)
MASKED = -1e30

VMEM = pl.BlockSpec(memory_space=pltpu.VMEM)
SMEM = pl.BlockSpec(memory_space=pltpu.SMEM)
HBM = pl.BlockSpec(memory_space=pltpu.HBM)


def partner(x, axis, apart):
    return lax.ppermute(x, axis, [(i, i ^ 1 << apart) for i in range(lax.axis_size(axis))])


def normalize(values):
    centered = values - jnp.mean(values, axis=-1, keepdims=True)
    variance = jnp.mean(centered * centered, axis=-1, keepdims=True)
    return centered * lax.rsqrt(variance + 1e-06)


def dot(left, right, dims):
    return lax.dot_general(left, right, (dims, ((), ())), preferred_element_type=jnp.float32)


def front_kernel(
    offsets,
    patches_hbm,
    row_hbm,
    col_hbm,
    weight_hbm,
    resid_hbm,
    queries,
    pairs,
    resid,
    patches,
    tables,
    weight,
    sems,
):
    rows = patches.shape[0]
    side = tables.shape[0] // 2
    copies = [
        pltpu.make_async_copy(row_hbm, tables.at[pl.ds(0, side), :], sems.at[0]),
        pltpu.make_async_copy(col_hbm, tables.at[pl.ds(side, side), :], sems.at[1]),
        pltpu.make_async_copy(patches_hbm, patches, sems.at[2]),
        pltpu.make_async_copy(weight_hbm, weight, sems.at[3]),
    ]
    for copy in copies:
        copy.start()
    place = lax.axis_index("tok")
    first = place // 2 * 2
    position = place * rows + lax.broadcasted_iota(jnp.int32, (rows, 2 * side), 0)
    start = jnp.where(position >= offsets[first + 1], offsets[first + 1], offsets[first])
    local = position - start
    window = local >> 2
    quarter = local & 3
    half = WIDTH // 2
    row = 2 * (window // half) + (quarter >> 1)
    col = 2 * (window % half) + (quarter & 1)
    lane = lax.broadcasted_iota(jnp.int32, (rows, 2 * side), 1)
    onehot = lane == jnp.where(lane < side, row, col + side)
    onehot = jnp.where(onehot, 1.0, 0.0).astype(jnp.bfloat16)
    copies[0].wait()
    copies[1].wait()
    embedded = dot(onehot, tables[...], ((1,), (0,)))
    copies[2].wait()
    values = patches[...].astype(jnp.float32) + embedded
    for tile in range(resid.shape[0]):
        resid[tile] = values[:, tile * LANES : (tile + 1) * LANES]
    resid_copy = pltpu.make_async_copy(resid, resid_hbm, sems.at[4])
    resid_copy.start()
    normed = normalize(values).astype(jnp.bfloat16)
    copies[3].wait()
    width = weight.shape[1]
    wide = weight[...].reshape(3 * width, weight.shape[2])
    out = dot(wide, normed, ((1,), (1,))).astype(jnp.bfloat16)
    queries[...] = out[:width]
    pairs[...] = out[width:]
    resid_copy.wait()


def attend_kernel(offsets, queries, near, far, out):
    rows = queries.shape[1]
    width = queries.shape[0]
    place = lax.axis_index("tok")
    core = place % 2
    border = offsets[place // 2 * 2 + 1]
    ahead = jnp.where(core == 0, rows, -rows)
    query_pos = place * rows + lax.broadcasted_iota(jnp.int32, (1, rows), 1)
    key_pos = place * rows + lax.broadcasted_iota(jnp.int32, (rows, 1), 0)
    query_side = jnp.where(query_pos >= border, 1, 0)
    near_side = jnp.where(key_pos >= border, 1, 0)
    far_side = jnp.where(key_pos + ahead >= border, 1, 0)
    for head in range(width // HEAD_DIM):
        own = slice(head * HEAD_DIM, (head + 1) * HEAD_DIM)
        value = slice(width + head * HEAD_DIM, width + (head + 1) * HEAD_DIM)
        query = queries[own, :]
        near_scores = dot(near[own, :], query, ((0,), (0,)))
        far_scores = dot(far[own, :], query, ((0,), (0,)))
        near_scores = jnp.where(near_side == query_side, near_scores * SCALE, MASKED)
        far_scores = jnp.where(far_side == query_side, far_scores * SCALE, MASKED)
        top = jnp.maximum(
            jnp.max(near_scores, axis=0, keepdims=True), jnp.max(far_scores, axis=0, keepdims=True)
        )
        near_expo = jnp.exp(near_scores - top)
        far_expo = jnp.exp(far_scores - top)
        total = jnp.sum(near_expo, axis=0, keepdims=True) + jnp.sum(far_expo, axis=0, keepdims=True)
        mixed = dot(near[value, :], near_expo.astype(jnp.bfloat16), ((1,), (0,)))
        mixed += dot(far[value, :], far_expo.astype(jnp.bfloat16), ((1,), (0,)))
        mixed = (mixed / total).astype(jnp.bfloat16)
        for copy in range(out.shape[0]):
            out[copy, own, :] = mixed


def merge_kernel(
    gathered,
    own_weight,
    other_hbm,
    resid_hbm,
    merge_hbm,
    out,
    other_weight,
    resid,
    merge_weight,
    total,
    sems,
):
    other_copy = pltpu.make_async_copy(other_hbm, other_weight, sems.at[0])
    resid_copy = pltpu.make_async_copy(resid_hbm, resid, sems.at[1])
    merge_copy = pltpu.make_async_copy(merge_hbm, merge_weight, sems.at[2])
    other_copy.start()
    resid_copy.start()
    merge_copy.start()
    core = lax.axis_index("tok") % 2
    group, depth, rows = gathered.shape
    attended = gathered[...].reshape(group * depth, rows)
    tiles = resid.shape[0]
    for weight, half in ((own_weight, core), (other_weight, 1 - core)):
        if weight is other_weight:
            other_copy.wait()
        part = dot(attended, weight[...], ((0,), (0,)))
        if weight is own_weight:
            resid_copy.wait()
        for tile in range(tiles // 2):
            place = half * (tiles // 2) + tile
            total[place] = resid[place] + part[:, tile * LANES : (tile + 1) * LANES]
    values = jnp.concatenate([total[tile] for tile in range(tiles)], axis=1)
    normed = normalize(values)
    for tile in range(tiles):
        total[tile] = normed[:, tile * LANES : (tile + 1) * LANES]
    width = tiles * LANES
    merge_copy.wait()
    projected = jnp.zeros(out.shape[1:], jnp.float32)
    for quarter in range(4):
        part = [total[tile, pl.ds(quarter, rows // 4, stride=4), :] for tile in range(tiles)]
        part = jnp.concatenate(part, axis=1).astype(jnp.bfloat16)
        weight = merge_weight[:, quarter * width : (quarter + 1) * width]
        projected += dot(weight, part, ((1,), (1,)))
    projected = projected.astype(out.dtype)
    for copy in range(out.shape[0]):
        out[copy] = projected


def pick_kernel(wanted, blocks, out):
    for slot in range(out.shape[0]):
        out[slot] = blocks[wanted[slot]]


def deliver_kernel(facts, blocks, out):
    source = 2 * facts[0]
    pair = jnp.concatenate([blocks[source], blocks[source + 1]], axis=1)
    shape = (pair.shape[1], out.shape[1])
    row = lax.broadcasted_iota(jnp.int32, shape, 0) - facts[1]
    slot = lax.broadcasted_iota(jnp.int32, shape, 1)
    chosen = row == jnp.where(slot < facts[2], slot, -shape[0])
    chosen = jnp.where(chosen, 1.0, 0.0).astype(jnp.bfloat16)
    out[...] = dot(pair, chosen, ((1,), (0,))).astype(out.dtype)


def on_device(
    patches,
    row_table,
    col_table,
    qkv_weight,
    out_weight,
    merge_weight,
    segment_ids,
    image_grids,
    image_offsets,
    owners,
):
    block_rows, width = patches.shape
    width_here = qkv_weight.shape[1]
    group = lax.axis_size("head")
    places = lax.axis_size("tok")
    place = lax.axis_index("tok")
    params = pltpu.CompilerParams(vmem_limit_bytes=24 * 2**20)
    at_hbm = lambda x: pltpu.with_memory_space_constraint(x, pltpu.HBM)

    sides = places // (RING * 2)
    tok_of = [[[(x * RING + y) * 2 + c for c in range(2)] for y in range(RING)] for x in range(sides)]
    rings_y = [[tok_of[x][y][c] for y in range(RING)] for x in range(sides) for c in range(2)]
    rings_x = [[tok_of[x][y][c] for x in range(sides)] for y in range(RING) for c in range(2)]
    planes = [[tok_of[x][y][c] for x in range(sides) for c in range(2)] for y in range(RING)]
    my_x = place // (2 * RING)
    my_y = place // 2 % RING
    core = place % 2

    depth, columns = width_here // sides, width // 2
    piece = lax.dynamic_slice(out_weight, (my_x * depth, core * columns), (depth, columns))
    pieces = jnp.broadcast_to(piece[None], (group, depth, columns))
    pieces = lax.all_to_all(pieces, "head", 0, 0, tiled=True)

    resid, queries, near = pl.pallas_call(
        front_kernel,
        out_shape=(
            pltpu.HBM((width // LANES, block_rows, LANES), jnp.float32),
            jax.ShapeDtypeStruct((width_here, block_rows), jnp.bfloat16),
            jax.ShapeDtypeStruct((2 * width_here, block_rows), jnp.bfloat16),
        ),
        in_specs=[SMEM, HBM, HBM, HBM, HBM],
        out_specs=(HBM, VMEM, VMEM),
        scratch_shapes=[
            pltpu.VMEM((width // LANES, block_rows, LANES), jnp.float32),
            pltpu.VMEM(patches.shape, jnp.bfloat16),
            pltpu.VMEM((2 * row_table.shape[0], width), jnp.bfloat16),
            pltpu.VMEM(qkv_weight.shape, jnp.bfloat16),
            pltpu.SemaphoreType.DMA((5,)),
        ],
        compiler_params=params,
        cost_estimate=pl.CostEstimate(
            flops=3 * 2 * block_rows * width * width_here, bytes_accessed=8 * 2**20, transcendentals=0
        ),
    )(image_offsets, *map(at_hbm, (patches, row_table, col_table, qkv_weight)))
    far = partner(near, "tok", 0)
    sent = pl.pallas_call(
        attend_kernel,
        out_shape=jax.ShapeDtypeStruct((group, width_here, block_rows), jnp.bfloat16),
        in_specs=[SMEM, VMEM, VMEM, VMEM],
        out_specs=VMEM,
        compiler_params=params,
    )(image_offsets, queries, near, far)
    pieces, sent = lax.optimization_barrier((pieces, sent))
    own_weight = lax.all_gather(pieces, "tok", axis=0, axis_index_groups=rings_x)
    own_weight = own_weight.transpose(1, 0, 2, 3).reshape(group * width_here, columns)
    other_weight = partner(own_weight, "tok", 0)

    gathered = lax.all_to_all(sent, "head", 0, 0, tiled=True)
    rows_here = block_rows // 4
    blocks_shape = jax.ShapeDtypeStruct((RING, width_here, rows_here), jnp.bfloat16)
    projected = pl.pallas_call(
        merge_kernel,
        out_shape=blocks_shape,
        in_specs=[VMEM, VMEM, HBM, HBM, HBM],
        out_specs=VMEM,
        scratch_shapes=[
            pltpu.VMEM(other_weight.shape, jnp.bfloat16),
            pltpu.VMEM((width // LANES, block_rows, LANES), jnp.float32),
            pltpu.VMEM(merge_weight.shape, jnp.bfloat16),
            pltpu.VMEM((width // LANES, block_rows, LANES), jnp.float32),
            pltpu.SemaphoreType.DMA((3,)),
        ],
        compiler_params=params,
    )(gathered, own_weight, *map(at_hbm, (other_weight, resid, merge_weight)))

    image_ids = jnp.arange(owners.shape[0], dtype=jnp.int32)
    place_ids = jnp.arange(places, dtype=jnp.int32)
    image_of = jnp.sum(jnp.where(owners[None, :] == place_ids[:, None], image_ids[None, :], 0), axis=1)
    pair_y = (image_of // 2 % RING).reshape(sides, RING, 2)
    wanted = jnp.sum(
        jnp.where((jnp.arange(RING) == my_y)[None, :, None], pair_y, 0), axis=1
    ).reshape(2 * sides)
    mine = owners == place
    tokens = image_grids[:, 0] * image_grids[:, 1]
    first_token = image_offsets - image_ids // 2 * (2 * block_rows)
    facts = jnp.stack([image_ids // 2 // RING, first_token // 4, tokens // 4])
    facts = jnp.sum(jnp.where(mine[None, :], facts, 0), axis=1)

    blocks = lax.all_to_all(projected, "tok", 0, 0, axis_index_groups=rings_y, tiled=True)
    blocks = pl.pallas_call(
        pick_kernel,
        out_shape=jax.ShapeDtypeStruct((2 * sides, width_here, rows_here), jnp.bfloat16),
        in_specs=[SMEM, VMEM],
        out_specs=VMEM,
        compiler_params=params,
    )(wanted, blocks)
    blocks = lax.all_to_all(blocks, "tok", 0, 0, axis_index_groups=planes, tiled=True)
    return pl.pallas_call(
        deliver_kernel,
        out_shape=jax.ShapeDtypeStruct((width_here, CAP), jnp.bfloat16),
        in_specs=[SMEM, VMEM],
        out_specs=VMEM,
        compiler_params=params,
    )(facts, blocks).T


def solution(mesh):
    placed = (
        P("tok", None),
        P(),
        P(),
        P(None, "head", None),
        P("head", None),
        P("head", None),
        P("tok"),
        P(),
        P(),
        P(),
    )
    return jax.shard_map(
        on_device, mesh=mesh, in_specs=placed, out_specs=P("tok", "head"), check_vma=False
    )
```

```python
import math

import jax
import jax.numpy as jnp
from jax import lax
from jax.experimental import pallas as pl
from jax.experimental.pallas import tpu as pltpu
from jax.sharding import PartitionSpec as P

HEAD_DIM = 80
CAP = 248
WIDTH = 16
LANES = 128
RING = 8
SCALE = 1.0 / math.sqrt(HEAD_DIM)
MASKED = -1e30

VMEM = pl.BlockSpec(memory_space=pltpu.VMEM)
SMEM = pl.BlockSpec(memory_space=pltpu.SMEM)
HBM = pl.BlockSpec(memory_space=pltpu.HBM)
ANY = pl.BlockSpec(memory_space=pl.ANY)


def partner(x, axis, apart):
    return lax.ppermute(x, axis, [(i, i ^ 1 << apart) for i in range(lax.axis_size(axis))])


def normalize(values):
    centered = values - jnp.mean(values, axis=-1, keepdims=True)
    variance = jnp.mean(centered * centered, axis=-1, keepdims=True)
    return centered * lax.rsqrt(variance + 1e-06)


def dot(left, right, dims):
    return lax.dot_general(left, right, (dims, ((), ())), preferred_element_type=jnp.float32)


def front_kernel(
    offsets_hbm,
    patches_hbm,
    row_hbm,
    col_hbm,
    weight_hbm,
    resid_hbm,
    queries,
    pairs,
    resid,
    patches,
    tables,
    weight,
    offsets,
    sems,
):
    rows = patches.shape[0]
    side = tables.shape[0] // 2
    copies = [
        pltpu.make_async_copy(row_hbm, tables.at[pl.ds(0, side), :], sems.at[0]),
        pltpu.make_async_copy(col_hbm, tables.at[pl.ds(side, side), :], sems.at[1]),
        pltpu.make_async_copy(patches_hbm, patches, sems.at[2]),
        pltpu.make_async_copy(weight_hbm, weight, sems.at[3]),
    ]
    offsets_copy = pltpu.make_async_copy(offsets_hbm, offsets, sems.at[5])
    offsets_copy.start()
    for copy in copies:
        copy.start()
    offsets_copy.wait()
    place = lax.axis_index("tok")
    first = place // 2 * 2
    position = place * rows + lax.broadcasted_iota(jnp.int32, (rows, 2 * side), 0)
    start = jnp.where(position >= offsets[first + 1], offsets[first + 1], offsets[first])
    local = position - start
    window = local >> 2
    quarter = local & 3
    half = WIDTH // 2
    row = 2 * (window // half) + (quarter >> 1)
    col = 2 * (window % half) + (quarter & 1)
    lane = lax.broadcasted_iota(jnp.int32, (rows, 2 * side), 1)
    onehot = lane == jnp.where(lane < side, row, col + side)
    onehot = jnp.where(onehot, 1.0, 0.0).astype(jnp.bfloat16)
    copies[0].wait()
    copies[1].wait()
    embedded = dot(onehot, tables[...], ((1,), (0,)))
    copies[2].wait()
    values = patches[...].astype(jnp.float32) + embedded
    for tile in range(resid.shape[0]):
        resid[tile] = values[:, tile * LANES : (tile + 1) * LANES]
    resid_copy = pltpu.make_async_copy(resid, resid_hbm, sems.at[4])
    resid_copy.start()
    normed = normalize(values).astype(jnp.bfloat16)
    copies[3].wait()
    width = weight.shape[1]
    wide = weight[...].reshape(3 * width, weight.shape[2])
    out = dot(wide, normed, ((1,), (1,))).astype(jnp.bfloat16)
    queries[...] = out[:width]
    pairs[...] = out[width:]
    resid_copy.wait()


def attend_kernel(offsets, queries, near, far, out):
    rows = queries.shape[1]
    width = queries.shape[0]
    place = lax.axis_index("tok")
    core = place % 2
    border = offsets[place // 2 * 2 + 1]
    ahead = jnp.where(core == 0, rows, -rows)
    query_pos = place * rows + lax.broadcasted_iota(jnp.int32, (1, rows), 1)
    key_pos = place * rows + lax.broadcasted_iota(jnp.int32, (rows, 1), 0)
    query_side = jnp.where(query_pos >= border, 1, 0)
    near_side = jnp.where(key_pos >= border, 1, 0)
    far_side = jnp.where(key_pos + ahead >= border, 1, 0)
    for head in range(width // HEAD_DIM):
        own = slice(head * HEAD_DIM, (head + 1) * HEAD_DIM)
        value = slice(width + head * HEAD_DIM, width + (head + 1) * HEAD_DIM)
        query = queries[own, :]
        near_scores = dot(near[own, :], query, ((0,), (0,)))
        far_scores = dot(far[own, :], query, ((0,), (0,)))
        near_scores = jnp.where(near_side == query_side, near_scores * SCALE, MASKED)
        far_scores = jnp.where(far_side == query_side, far_scores * SCALE, MASKED)
        top = jnp.maximum(
            jnp.max(near_scores, axis=0, keepdims=True), jnp.max(far_scores, axis=0, keepdims=True)
        )
        near_expo = jnp.exp(near_scores - top)
        far_expo = jnp.exp(far_scores - top)
        total = jnp.sum(near_expo, axis=0, keepdims=True) + jnp.sum(far_expo, axis=0, keepdims=True)
        mixed = dot(near[value, :], near_expo.astype(jnp.bfloat16), ((1,), (0,)))
        mixed += dot(far[value, :], far_expo.astype(jnp.bfloat16), ((1,), (0,)))
        mixed = (mixed / total).astype(jnp.bfloat16)
        for copy in range(out.shape[0]):
            out[copy, own, :] = mixed


def piece_kernel(weight, out, sems):
    depth, columns = out.shape[1:]
    place = lax.axis_index("tok")
    row = pl.multiple_of(place // (2 * RING) * depth, 8)
    column = pl.multiple_of(place % 2 * columns, LANES)
    copies = [
        pltpu.make_async_copy(
            weight.at[pl.ds(row, depth), pl.ds(column, columns)], out.at[copy], sems.at[copy]
        )
        for copy in range(out.shape[0])
    ]
    for copy in copies:
        copy.start()
    for copy in copies:
        copy.wait()


def project_kernel(gathered, weight, resid_hbm, attended, partial, resid, sem):
    resid_copy = pltpu.make_async_copy(resid_hbm, resid, sem)
    resid_copy.start()
    core = lax.axis_index("tok") % 2
    group, depth, rows = gathered.shape
    whole = gathered[...].reshape(group * depth, rows)
    tiles = resid.shape[0]
    for tile in range(tiles):
        part = slice(tile * LANES, (tile + 1) * LANES)
        attended[:, part] = whole[part, :].T
    part = dot(attended[...], weight[...], ((1,), (0,)))
    resid_copy.wait()
    for tile in range(tiles // 2):
        place = core * (tiles // 2) + tile
        partial[place] = resid[place] + part[:, tile * LANES : (tile + 1) * LANES]
        place = (1 - core) * (tiles // 2) + tile
        partial[place] = resid[place]


def merge_kernel(attended, weight, partial, merge_hbm, out, merge_weight, total, sem):
    merge_copy = pltpu.make_async_copy(merge_hbm, merge_weight, sem)
    merge_copy.start()
    core = lax.axis_index("tok") % 2
    tiles, rows = partial.shape[:2]
    part = dot(attended[...], weight[...], ((1,), (0,)))
    for tile in range(tiles // 2):
        place = core * (tiles // 2) + tile
        total[place] = partial[place]
        place = (1 - core) * (tiles // 2) + tile
        total[place] = partial[place] + part[:, tile * LANES : (tile + 1) * LANES]
    values = jnp.concatenate([total[tile] for tile in range(tiles)], axis=1)
    normed = normalize(values)
    for tile in range(tiles):
        total[tile] = normed[:, tile * LANES : (tile + 1) * LANES]
    width = tiles * LANES
    merge_copy.wait()
    projected = jnp.zeros(out.shape[1:], jnp.float32)
    for quarter in range(4):
        part = [total[tile, pl.ds(quarter, rows // 4, stride=4), :] for tile in range(tiles)]
        part = jnp.concatenate(part, axis=1).astype(jnp.bfloat16)
        weight = merge_weight[:, quarter * width : (quarter + 1) * width]
        projected += dot(weight, part, ((1,), (1,)))
    projected = projected.astype(out.dtype)
    for copy in range(out.shape[0]):
        out[copy] = projected


def pick_kernel(wanted, blocks, out, sems):
    copies = [
        pltpu.make_async_copy(blocks.at[wanted[slot]], out.at[slot], sems.at[slot])
        for slot in range(out.shape[0])
    ]
    for copy in copies:
        copy.start()
    for copy in copies:
        copy.wait()


def deliver_kernel(facts, blocks, out):
    source = 2 * facts[0]
    pair = jnp.concatenate([blocks[source], blocks[source + 1]], axis=1)
    shape = (pair.shape[1], out.shape[1])
    row = lax.broadcasted_iota(jnp.int32, shape, 0) - facts[1]
    slot = lax.broadcasted_iota(jnp.int32, shape, 1)
    chosen = row == jnp.where(slot < facts[2], slot, -shape[0])
    chosen = jnp.where(chosen, 1.0, 0.0).astype(jnp.bfloat16)
    out[...] = dot(pair, chosen, ((1,), (0,))).astype(out.dtype)


def on_device(
    patches,
    row_table,
    col_table,
    qkv_weight,
    out_weight,
    merge_weight,
    segment_ids,
    image_grids,
    image_offsets,
    owners,
):
    block_rows, width = patches.shape
    width_here = qkv_weight.shape[1]
    group = lax.axis_size("head")
    places = lax.axis_size("tok")
    place = lax.axis_index("tok")
    params = pltpu.CompilerParams(vmem_limit_bytes=24 * 2**20)
    at_hbm = lambda x: pltpu.with_memory_space_constraint(x, pltpu.HBM)

    sides = places // (RING * 2)
    tok_of = [[[(x * RING + y) * 2 + c for c in range(2)] for y in range(RING)] for x in range(sides)]
    rings_y = [[tok_of[x][y][c] for y in range(RING)] for x in range(sides) for c in range(2)]
    rings_x = [[tok_of[x][y][c] for x in range(sides)] for y in range(RING) for c in range(2)]
    planes = [[tok_of[x][y][c] for x in range(sides) for c in range(2)] for y in range(RING)]
    my_x = place // (2 * RING)
    my_y = place // 2 % RING
    core = place % 2

    depth, columns = width_here // sides, width // 2
    pieces = pl.pallas_call(
        piece_kernel,
        out_shape=pltpu.HBM((group, depth, columns), jnp.bfloat16),
        in_specs=[HBM],
        out_specs=HBM,
        scratch_shapes=[pltpu.SemaphoreType.DMA((group,))],
        compiler_params=params,
    )(at_hbm(out_weight))
    pieces = lax.all_to_all(pieces, "head", 0, 0, tiled=True)

    resid, queries, near = pl.pallas_call(
        front_kernel,
        out_shape=(
            pltpu.HBM((width // LANES, block_rows, LANES), jnp.float32),
            jax.ShapeDtypeStruct((width_here, block_rows), jnp.bfloat16),
            jax.ShapeDtypeStruct((2 * width_here, block_rows), jnp.bfloat16),
        ),
        in_specs=[HBM] * 5,
        out_specs=(HBM, VMEM, VMEM),
        scratch_shapes=[
            pltpu.VMEM((width // LANES, block_rows, LANES), jnp.float32),
            pltpu.VMEM(patches.shape, jnp.bfloat16),
            pltpu.VMEM((2 * row_table.shape[0], width), jnp.bfloat16),
            pltpu.VMEM(qkv_weight.shape, jnp.bfloat16),
            pltpu.SMEM(image_offsets.shape, jnp.int32),
            pltpu.SemaphoreType.DMA((6,)),
        ],
        compiler_params=params,
        cost_estimate=pl.CostEstimate(
            flops=3 * 2 * block_rows * width * width_here, bytes_accessed=8 * 2**20, transcendentals=0
        ),
    )(*map(at_hbm, (image_offsets, patches, row_table, col_table, qkv_weight)))
    far = partner(near, "tok", 0)
    sent = pl.pallas_call(
        attend_kernel,
        out_shape=jax.ShapeDtypeStruct((group, width_here, block_rows), jnp.bfloat16),
        in_specs=[SMEM, VMEM, VMEM, VMEM],
        out_specs=VMEM,
        compiler_params=params,
    )(image_offsets, queries, near, far)
    pieces, sent = lax.optimization_barrier((pieces, sent))
    own_weight = lax.all_gather(pieces, "tok", axis=0, axis_index_groups=rings_x)
    own_weight = own_weight.transpose(1, 0, 2, 3).reshape(group * width_here, columns)
    other_weight = partner(own_weight, "tok", 0)

    gathered = lax.all_to_all(sent, "head", 0, 0, tiled=True)
    rows_here = block_rows // 4
    blocks_shape = jax.ShapeDtypeStruct((RING, width_here, rows_here), jnp.bfloat16)
    tiles = width // LANES
    half_flops = 2 * block_rows * width * columns
    attended, partial = pl.pallas_call(
        project_kernel,
        out_shape=(
            jax.ShapeDtypeStruct((block_rows, width), jnp.bfloat16),
            jax.ShapeDtypeStruct((tiles, block_rows, LANES), jnp.float32),
        ),
        in_specs=[VMEM, VMEM, HBM],
        out_specs=(VMEM, VMEM),
        scratch_shapes=[
            pltpu.VMEM((tiles, block_rows, LANES), jnp.float32),
            pltpu.SemaphoreType.DMA,
        ],
        compiler_params=params,
        cost_estimate=pl.CostEstimate(
            flops=half_flops, bytes_accessed=8 * 2**20, transcendentals=0
        ),
    )(gathered, own_weight, at_hbm(resid))
    projected = pl.pallas_call(
        merge_kernel,
        out_shape=blocks_shape,
        in_specs=[VMEM, VMEM, VMEM, HBM],
        out_specs=VMEM,
        scratch_shapes=[
            pltpu.VMEM(merge_weight.shape, jnp.bfloat16),
            pltpu.VMEM((tiles, block_rows, LANES), jnp.float32),
            pltpu.SemaphoreType.DMA,
        ],
        compiler_params=params,
    )(attended, other_weight, partial, at_hbm(merge_weight))

    image_ids = jnp.arange(owners.shape[0], dtype=jnp.int32)
    place_ids = jnp.arange(places, dtype=jnp.int32)
    image_of = jnp.sum(jnp.where(owners[None, :] == place_ids[:, None], image_ids[None, :], 0), axis=1)
    pair_y = (image_of // 2 % RING).reshape(sides, RING, 2)
    wanted = jnp.sum(
        jnp.where((jnp.arange(RING) == my_y)[None, :, None], pair_y, 0), axis=1
    ).reshape(2 * sides)
    mine = owners == place
    tokens = image_grids[:, 0] * image_grids[:, 1]
    first_token = image_offsets - image_ids // 2 * (2 * block_rows)
    facts = jnp.stack([image_ids // 2 // RING, first_token // 4, tokens // 4])
    facts = jnp.sum(jnp.where(mine[None, :], facts, 0), axis=1)

    blocks = lax.all_to_all(projected, "tok", 0, 0, axis_index_groups=rings_y, tiled=True)
    blocks = pl.pallas_call(
        pick_kernel,
        out_shape=pltpu.HBM((2 * sides, width_here, rows_here), jnp.bfloat16),
        in_specs=[SMEM, ANY],
        out_specs=HBM,
        scratch_shapes=[pltpu.SemaphoreType.DMA((2 * sides,))],
        compiler_params=params,
    )(wanted, blocks)
    blocks = lax.all_to_all(blocks, "tok", 0, 0, axis_index_groups=planes, tiled=True)
    return pl.pallas_call(
        deliver_kernel,
        out_shape=jax.ShapeDtypeStruct((width_here, CAP), jnp.bfloat16),
        in_specs=[SMEM, VMEM],
        out_specs=VMEM,
        compiler_params=params,
    )(facts, blocks).T


def solution(mesh):
    placed = (
        P("tok", None),
        P(),
        P(),
        P(None, "head", None),
        P("head", None),
        P("head", None),
        P("tok"),
        P(),
        P(),
        P(),
    )
    return jax.shard_map(
        on_device, mesh=mesh, in_specs=placed, out_specs=P("tok", "head"), check_vma=False
    )
```

```python
import math

import jax
import jax.numpy as jnp
from jax import lax
from jax.experimental import pallas as pl
from jax.experimental.pallas import tpu as pltpu
from jax.sharding import PartitionSpec as P

HEAD_DIM = 80
CAP = 248
WIDTH = 16
LANES = 128
RING = 8
SCALE = 1.0 / math.sqrt(HEAD_DIM)
MASKED = -1e30

VMEM = pl.BlockSpec(memory_space=pltpu.VMEM)
SMEM = pl.BlockSpec(memory_space=pltpu.SMEM)
HBM = pl.BlockSpec(memory_space=pltpu.HBM)
ANY = pl.BlockSpec(memory_space=pl.ANY)


def partner(x, axis, apart):
    return lax.ppermute(x, axis, [(i, i ^ 1 << apart) for i in range(lax.axis_size(axis))])


def normalize(values):
    centered = values - jnp.mean(values, axis=-1, keepdims=True)
    variance = jnp.mean(centered * centered, axis=-1, keepdims=True)
    return centered * lax.rsqrt(variance + 1e-06)


def dot(left, right, dims):
    return lax.dot_general(left, right, (dims, ((), ())), preferred_element_type=jnp.float32)


def front_kernel(
    offsets_hbm,
    patches_hbm,
    row_hbm,
    col_hbm,
    weight_hbm,
    resid_hbm,
    queries,
    pairs,
    resid,
    patches,
    tables,
    weight,
    offsets,
    sems,
):
    rows = patches.shape[0]
    side = tables.shape[0] // 2
    copies = [
        pltpu.make_async_copy(row_hbm, tables.at[pl.ds(0, side), :], sems.at[0]),
        pltpu.make_async_copy(col_hbm, tables.at[pl.ds(side, side), :], sems.at[1]),
        pltpu.make_async_copy(patches_hbm, patches, sems.at[2]),
        pltpu.make_async_copy(weight_hbm, weight, sems.at[3]),
    ]
    offsets_copy = pltpu.make_async_copy(offsets_hbm, offsets, sems.at[5])
    offsets_copy.start()
    for copy in copies:
        copy.start()
    offsets_copy.wait()
    place = lax.axis_index("tok")
    first = place // 2 * 2
    position = place * rows + lax.broadcasted_iota(jnp.int32, (rows, 2 * side), 0)
    start = jnp.where(position >= offsets[first + 1], offsets[first + 1], offsets[first])
    local = position - start
    window = local >> 2
    quarter = local & 3
    half = WIDTH // 2
    row = 2 * (window // half) + (quarter >> 1)
    col = 2 * (window % half) + (quarter & 1)
    lane = lax.broadcasted_iota(jnp.int32, (rows, 2 * side), 1)
    onehot = lane == jnp.where(lane < side, row, col + side)
    onehot = jnp.where(onehot, 1.0, 0.0).astype(jnp.bfloat16)
    copies[0].wait()
    copies[1].wait()
    embedded = dot(onehot, tables[...], ((1,), (0,)))
    copies[2].wait()
    values = patches[...].astype(jnp.float32) + embedded
    for tile in range(resid.shape[0]):
        resid[tile] = values[:, tile * LANES : (tile + 1) * LANES]
    resid_copy = pltpu.make_async_copy(resid, resid_hbm, sems.at[4])
    resid_copy.start()
    normed = normalize(values).astype(jnp.bfloat16)
    copies[3].wait()
    width = weight.shape[1]
    wide = weight[...].reshape(3 * width, weight.shape[2])
    out = dot(wide, normed, ((1,), (1,))).astype(jnp.bfloat16)
    queries[...] = out[:width]
    pairs[...] = out[width:]
    resid_copy.wait()


def attend_kernel(offsets, queries, near, far, out):
    rows = queries.shape[1]
    width = queries.shape[0]
    place = lax.axis_index("tok")
    core = place % 2
    border = offsets[place // 2 * 2 + 1]
    ahead = jnp.where(core == 0, rows, -rows)
    query_pos = place * rows + lax.broadcasted_iota(jnp.int32, (1, rows), 1)
    key_pos = place * rows + lax.broadcasted_iota(jnp.int32, (rows, 1), 0)
    query_side = jnp.where(query_pos >= border, 1, 0)
    near_side = jnp.where(key_pos >= border, 1, 0)
    far_side = jnp.where(key_pos + ahead >= border, 1, 0)
    for head in range(width // HEAD_DIM):
        own = slice(head * HEAD_DIM, (head + 1) * HEAD_DIM)
        value = slice(width + head * HEAD_DIM, width + (head + 1) * HEAD_DIM)
        query = queries[own, :]
        near_scores = dot(near[own, :], query, ((0,), (0,)))
        far_scores = dot(far[own, :], query, ((0,), (0,)))
        near_scores = jnp.where(near_side == query_side, near_scores * SCALE, MASKED)
        far_scores = jnp.where(far_side == query_side, far_scores * SCALE, MASKED)
        top = jnp.maximum(
            jnp.max(near_scores, axis=0, keepdims=True), jnp.max(far_scores, axis=0, keepdims=True)
        )
        near_expo = jnp.exp(near_scores - top)
        far_expo = jnp.exp(far_scores - top)
        total = jnp.sum(near_expo, axis=0, keepdims=True) + jnp.sum(far_expo, axis=0, keepdims=True)
        mixed = dot(near[value, :], near_expo.astype(jnp.bfloat16), ((1,), (0,)))
        mixed += dot(far[value, :], far_expo.astype(jnp.bfloat16), ((1,), (0,)))
        mixed = (mixed / total).astype(jnp.bfloat16)
        for copy in range(out.shape[0]):
            out[copy, own, :] = mixed


def project_kernel(
    gathered, weight, resid_hbm, merge_hbm, attended, partial, merge_weight, resid, sems
):
    resid_copy = pltpu.make_async_copy(resid_hbm, resid, sems.at[0])
    resid_copy.start()
    merge_copy = pltpu.make_async_copy(merge_hbm, merge_weight, sems.at[1])
    merge_copy.start()
    core = lax.axis_index("tok") % 2
    group, depth, rows = gathered.shape
    whole = gathered[...].reshape(group * depth, rows)
    tiles = resid.shape[0]
    for tile in range(tiles):
        part = slice(tile * LANES, (tile + 1) * LANES)
        attended[:, part] = whole[part, :].T
    part = dot(attended[...], weight[...], ((1,), (0,)))
    resid_copy.wait()
    for tile in range(tiles // 2):
        place = core * (tiles // 2) + tile
        partial[place] = resid[place] + part[:, tile * LANES : (tile + 1) * LANES]
        place = (1 - core) * (tiles // 2) + tile
        partial[place] = resid[place]
    merge_copy.wait()


def merge_kernel(attended, weight, partial, merge_weight, out, total):
    core = lax.axis_index("tok") % 2
    tiles, rows = partial.shape[:2]
    part = dot(attended[...], weight[...], ((1,), (0,)))
    for tile in range(tiles // 2):
        place = core * (tiles // 2) + tile
        total[place] = partial[place]
        place = (1 - core) * (tiles // 2) + tile
        total[place] = partial[place] + part[:, tile * LANES : (tile + 1) * LANES]
    values = jnp.concatenate([total[tile] for tile in range(tiles)], axis=1)
    normed = normalize(values)
    for tile in range(tiles):
        total[tile] = normed[:, tile * LANES : (tile + 1) * LANES]
    width = tiles * LANES
    projected = jnp.zeros(out.shape[1:], jnp.float32)
    for quarter in range(4):
        part = [total[tile, pl.ds(quarter, rows // 4, stride=4), :] for tile in range(tiles)]
        part = jnp.concatenate(part, axis=1).astype(jnp.bfloat16)
        weight = merge_weight[:, quarter * width : (quarter + 1) * width]
        projected += dot(weight, part, ((1,), (1,)))
    projected = projected.astype(out.dtype)
    for copy in range(out.shape[0]):
        out[copy] = projected


def pick_kernel(wanted, blocks, out, sems):
    copies = [
        pltpu.make_async_copy(blocks.at[wanted[slot]], out.at[slot], sems.at[slot])
        for slot in range(out.shape[0])
    ]
    for copy in copies:
        copy.start()
    for copy in copies:
        copy.wait()


def deliver_kernel(facts, blocks, out):
    source = 2 * facts[0]
    pair = jnp.concatenate([blocks[source], blocks[source + 1]], axis=1)
    shape = (pair.shape[1], out.shape[1])
    row = lax.broadcasted_iota(jnp.int32, shape, 0) - facts[1]
    slot = lax.broadcasted_iota(jnp.int32, shape, 1)
    chosen = row == jnp.where(slot < facts[2], slot, -shape[0])
    chosen = jnp.where(chosen, 1.0, 0.0).astype(jnp.bfloat16)
    out[...] = dot(pair, chosen, ((1,), (0,))).astype(out.dtype)


def on_device(
    patches,
    row_table,
    col_table,
    qkv_weight,
    out_weight,
    merge_weight,
    segment_ids,
    image_grids,
    image_offsets,
    owners,
):
    block_rows, width = patches.shape
    width_here = qkv_weight.shape[1]
    group = lax.axis_size("head")
    places = lax.axis_size("tok")
    place = lax.axis_index("tok")
    params = pltpu.CompilerParams(vmem_limit_bytes=24 * 2**20)
    at_hbm = lambda x: pltpu.with_memory_space_constraint(x, pltpu.HBM)

    sides = places // (RING * 2)
    tok_of = [[[(x * RING + y) * 2 + c for c in range(2)] for y in range(RING)] for x in range(sides)]
    rings_y = [[tok_of[x][y][c] for y in range(RING)] for x in range(sides) for c in range(2)]
    rings_x = [[tok_of[x][y][c] for x in range(sides)] for y in range(RING) for c in range(2)]
    planes = [[tok_of[x][y][c] for x in range(sides) for c in range(2)] for y in range(RING)]
    my_x = place // (2 * RING)
    my_y = place // 2 % RING
    core = place % 2

    depth, columns = width_here // sides, width // 2
    piece = lax.dynamic_slice(out_weight, (my_x * depth, core * columns), (depth, columns))
    pieces = jnp.broadcast_to(piece[None], (group, depth, columns))
    pieces = lax.all_to_all(pieces, "head", 0, 0, tiled=True)

    resid, queries, near = pl.pallas_call(
        front_kernel,
        out_shape=(
            pltpu.HBM((width // LANES, block_rows, LANES), jnp.float32),
            jax.ShapeDtypeStruct((width_here, block_rows), jnp.bfloat16),
            jax.ShapeDtypeStruct((2 * width_here, block_rows), jnp.bfloat16),
        ),
        in_specs=[HBM] * 5,
        out_specs=(HBM, VMEM, VMEM),
        scratch_shapes=[
            pltpu.VMEM((width // LANES, block_rows, LANES), jnp.float32),
            pltpu.VMEM(patches.shape, jnp.bfloat16),
            pltpu.VMEM((2 * row_table.shape[0], width), jnp.bfloat16),
            pltpu.VMEM(qkv_weight.shape, jnp.bfloat16),
            pltpu.SMEM(image_offsets.shape, jnp.int32),
            pltpu.SemaphoreType.DMA((6,)),
        ],
        compiler_params=params,
        cost_estimate=pl.CostEstimate(
            flops=3 * 2 * block_rows * width * width_here, bytes_accessed=8 * 2**20, transcendentals=0
        ),
    )(*map(at_hbm, (image_offsets, patches, row_table, col_table, qkv_weight)))
    far = partner(near, "tok", 0)
    sent = pl.pallas_call(
        attend_kernel,
        out_shape=jax.ShapeDtypeStruct((group, width_here, block_rows), jnp.bfloat16),
        in_specs=[SMEM, VMEM, VMEM, VMEM],
        out_specs=VMEM,
        compiler_params=params,
    )(image_offsets, queries, near, far)
    pieces, sent = lax.optimization_barrier((pieces, sent))
    own_weight = lax.all_gather(pieces, "tok", axis=0, axis_index_groups=rings_x)
    own_weight = own_weight.transpose(1, 0, 2, 3).reshape(group * width_here, columns)
    other_weight = partner(own_weight, "tok", 0)

    gathered = lax.all_to_all(sent, "head", 0, 0, tiled=True)
    rows_here = block_rows // 4
    blocks_shape = jax.ShapeDtypeStruct((RING, width_here, rows_here), jnp.bfloat16)
    tiles = width // LANES
    half_flops = 2 * block_rows * width * columns
    attended, partial, merge_here = pl.pallas_call(
        project_kernel,
        out_shape=(
            jax.ShapeDtypeStruct((block_rows, width), jnp.bfloat16),
            jax.ShapeDtypeStruct((tiles, block_rows, LANES), jnp.float32),
            jax.ShapeDtypeStruct(merge_weight.shape, jnp.bfloat16),
        ),
        in_specs=[VMEM, VMEM, HBM, HBM],
        out_specs=(VMEM, VMEM, VMEM),
        scratch_shapes=[
            pltpu.VMEM((tiles, block_rows, LANES), jnp.float32),
            pltpu.SemaphoreType.DMA((2,)),
        ],
        compiler_params=params,
        cost_estimate=pl.CostEstimate(
            flops=half_flops, bytes_accessed=8 * 2**20, transcendentals=0
        ),
    )(gathered, own_weight, at_hbm(resid), at_hbm(merge_weight))
    projected = pl.pallas_call(
        merge_kernel,
        out_shape=blocks_shape,
        in_specs=[VMEM, VMEM, VMEM, VMEM],
        out_specs=VMEM,
        scratch_shapes=[pltpu.VMEM((tiles, block_rows, LANES), jnp.float32)],
        compiler_params=params,
    )(attended, other_weight, partial, merge_here)

    image_ids = jnp.arange(owners.shape[0], dtype=jnp.int32)
    place_ids = jnp.arange(places, dtype=jnp.int32)
    image_of = jnp.sum(jnp.where(owners[None, :] == place_ids[:, None], image_ids[None, :], 0), axis=1)
    pair_y = (image_of // 2 % RING).reshape(sides, RING, 2)
    wanted = jnp.sum(
        jnp.where((jnp.arange(RING) == my_y)[None, :, None], pair_y, 0), axis=1
    ).reshape(2 * sides)
    mine = owners == place
    tokens = image_grids[:, 0] * image_grids[:, 1]
    first_token = image_offsets - image_ids // 2 * (2 * block_rows)
    facts = jnp.stack([image_ids // 2 // RING, first_token // 4, tokens // 4])
    facts = jnp.sum(jnp.where(mine[None, :], facts, 0), axis=1)

    blocks = lax.all_to_all(projected, "tok", 0, 0, axis_index_groups=rings_y, tiled=True)
    blocks = pl.pallas_call(
        pick_kernel,
        out_shape=pltpu.HBM((2 * sides, width_here, rows_here), jnp.bfloat16),
        in_specs=[SMEM, ANY],
        out_specs=HBM,
        scratch_shapes=[pltpu.SemaphoreType.DMA((2 * sides,))],
        compiler_params=params,
    )(wanted, blocks)
    blocks = lax.all_to_all(blocks, "tok", 0, 0, axis_index_groups=planes, tiled=True)
    return pl.pallas_call(
        deliver_kernel,
        out_shape=jax.ShapeDtypeStruct((width_here, CAP), jnp.bfloat16),
        in_specs=[SMEM, VMEM],
        out_specs=VMEM,
        compiler_params=params,
    )(facts, blocks).T


def solution(mesh):
    placed = (
        P("tok", None),
        P(),
        P(),
        P(None, "head", None),
        P("head", None),
        P("head", None),
        P("tok"),
        P(),
        P(),
        P(),
    )
    return jax.shard_map(
        on_device, mesh=mesh, in_specs=placed, out_specs=P("tok", "head"), check_vma=False
    )
```

```python
import math

import jax
import jax.numpy as jnp
from jax import lax
from jax.experimental import pallas as pl
from jax.experimental.pallas import tpu as pltpu
from jax.sharding import PartitionSpec as P

HEAD_DIM = 80
CAP = 248
WIDTH = 16
LANES = 128
RING = 8
SCALE = 1.0 / math.sqrt(HEAD_DIM)
MASKED = -1e30

VMEM = pl.BlockSpec(memory_space=pltpu.VMEM)
SMEM = pl.BlockSpec(memory_space=pltpu.SMEM)
HBM = pl.BlockSpec(memory_space=pltpu.HBM)
ANY = pl.BlockSpec(memory_space=pl.ANY)


def partner(x, axis, apart):
    return lax.ppermute(x, axis, [(i, i ^ 1 << apart) for i in range(lax.axis_size(axis))])


def normalize(values):
    centered = values - jnp.mean(values, axis=-1, keepdims=True)
    variance = jnp.mean(centered * centered, axis=-1, keepdims=True)
    return centered * lax.rsqrt(variance + 1e-06)


def dot(left, right, dims):
    return lax.dot_general(left, right, (dims, ((), ())), preferred_element_type=jnp.float32)


def front_kernel(
    offsets_hbm,
    patches,
    row_hbm,
    col_hbm,
    weight_hbm,
    resid_hbm,
    queries,
    pairs,
    resid,
    tables,
    weight,
    offsets,
    sems,
):
    rows = patches.shape[0]
    side = tables.shape[0] // 2
    copies = [
        pltpu.make_async_copy(row_hbm, tables.at[pl.ds(0, side), :], sems.at[0]),
        pltpu.make_async_copy(col_hbm, tables.at[pl.ds(side, side), :], sems.at[1]),
        pltpu.make_async_copy(weight_hbm, weight, sems.at[2]),
    ]
    offsets_copy = pltpu.make_async_copy(offsets_hbm, offsets, sems.at[4])
    offsets_copy.start()
    for copy in copies:
        copy.start()
    offsets_copy.wait()
    place = lax.axis_index("tok")
    first = place // 2 * 2
    position = place * rows + lax.broadcasted_iota(jnp.int32, (rows, 2 * side), 0)
    start = jnp.where(position >= offsets[first + 1], offsets[first + 1], offsets[first])
    local = position - start
    window = local >> 2
    quarter = local & 3
    half = WIDTH // 2
    row = 2 * (window // half) + (quarter >> 1)
    col = 2 * (window % half) + (quarter & 1)
    lane = lax.broadcasted_iota(jnp.int32, (rows, 2 * side), 1)
    onehot = lane == jnp.where(lane < side, row, col + side)
    onehot = jnp.where(onehot, 1.0, 0.0).astype(jnp.bfloat16)
    copies[0].wait()
    copies[1].wait()
    embedded = dot(onehot, tables[...], ((1,), (0,)))
    values = patches[...].astype(jnp.float32) + embedded
    for tile in range(resid.shape[0]):
        resid[tile] = values[:, tile * LANES : (tile + 1) * LANES]
    resid_copy = pltpu.make_async_copy(resid, resid_hbm, sems.at[3])
    resid_copy.start()
    normed = normalize(values).astype(jnp.bfloat16)
    copies[2].wait()
    width = weight.shape[1]
    wide = weight[...].reshape(3 * width, weight.shape[2])
    out = dot(wide, normed, ((1,), (1,))).astype(jnp.bfloat16)
    queries[...] = out[:width]
    pairs[...] = out[width:]
    resid_copy.wait()


def block_scores(offsets, block, query, other):
    rows = query.shape[1]
    place = lax.axis_index("tok")
    border = offsets[place // 2 * 2 + 1]
    key_place = jnp.where(place % 2 == 0, place + 1, place - 1) if other else place
    query_pos = place * rows + lax.broadcasted_iota(jnp.int32, (1, rows), 1)
    key_pos = key_place * rows + lax.broadcasted_iota(jnp.int32, (rows, 1), 0)
    query_side = jnp.where(query_pos >= border, 1, 0)
    key_side = jnp.where(key_pos >= border, 1, 0)
    scores = dot(block, query, ((0,), (0,))) * SCALE
    return jnp.where(key_side == query_side, scores, MASKED)


def near_kernel(offsets, queries, near, mixed, stats):
    width = queries.shape[0]
    for head in range(width // HEAD_DIM):
        own = slice(head * HEAD_DIM, (head + 1) * HEAD_DIM)
        value = slice(width + head * HEAD_DIM, width + (head + 1) * HEAD_DIM)
        scores = block_scores(offsets, near[own, :], queries[own, :], False)
        top = jnp.max(scores, axis=0, keepdims=True)
        expo = jnp.exp(scores - top)
        stats[2 * head : 2 * head + 1, :] = top
        stats[2 * head + 1 : 2 * head + 2, :] = jnp.sum(expo, axis=0, keepdims=True)
        mixed[own, :] = dot(near[value, :], expo.astype(jnp.bfloat16), ((1,), (0,)))


def far_kernel(offsets, queries, far, near_mixed, stats, out, attended, sems):
    width = queries.shape[0]
    copies = []
    for head in range(width // HEAD_DIM):
        own = slice(head * HEAD_DIM, (head + 1) * HEAD_DIM)
        value = slice(width + head * HEAD_DIM, width + (head + 1) * HEAD_DIM)
        scores = block_scores(offsets, far[own, :], queries[own, :], True)
        near_top = stats[2 * head : 2 * head + 1, :]
        top = jnp.maximum(near_top, jnp.max(scores, axis=0, keepdims=True))
        expo = jnp.exp(scores - top)
        scale = jnp.exp(near_top - top)
        total = stats[2 * head + 1 : 2 * head + 2, :] * scale
        total += jnp.sum(expo, axis=0, keepdims=True)
        mixed = near_mixed[own, :] * scale
        mixed += dot(far[value, :], expo.astype(jnp.bfloat16), ((1,), (0,)))
        attended[own, :] = (mixed / total).astype(jnp.bfloat16)
        part = pl.ds(head * HEAD_DIM, HEAD_DIM)
        for copy in range(out.shape[0]):
            copies.append(
                pltpu.make_async_copy(
                    attended.at[part, :], out.at[copy, part, :], sems.at[head, copy]
                )
            )
            copies[-1].start()
    for copy in copies:
        copy.wait()


def project_kernel(
    gathered, weight, resid_hbm, merge_hbm, attended, partial, merge_weight, resid, sems
):
    resid_copy = pltpu.make_async_copy(resid_hbm, resid, sems.at[0])
    resid_copy.start()
    merge_copy = pltpu.make_async_copy(merge_hbm, merge_weight, sems.at[1])
    merge_copy.start()
    core = lax.axis_index("tok") % 2
    group, depth, rows = gathered.shape
    whole = gathered[...].reshape(group * depth, rows)
    tiles = resid.shape[0]
    for tile in range(tiles):
        part = slice(tile * LANES, (tile + 1) * LANES)
        attended[:, part] = whole[part, :].T
    part = dot(attended[...], weight[...], ((1,), (0,)))
    resid_copy.wait()
    for tile in range(tiles // 2):
        place = core * (tiles // 2) + tile
        partial[place] = resid[place] + part[:, tile * LANES : (tile + 1) * LANES]
        place = (1 - core) * (tiles // 2) + tile
        partial[place] = resid[place]
    merge_copy.wait()


def merge_kernel(
    attended, weight_hbm, partial, merge_weight, out, weight, total, block, weight_sems, sems
):
    chunks = [(start, min(256, weight.shape[1] - start)) for start in range(0, weight.shape[1], 256)]
    loads = [
        pltpu.make_async_copy(
            weight_hbm.at[:, pl.ds(start, size)],
            weight.at[:, pl.ds(start, size)],
            weight_sems.at[chunk],
        )
        for chunk, (start, size) in enumerate(chunks)
    ]
    for load in loads:
        load.start()
    core = lax.axis_index("tok") % 2
    tiles, rows = partial.shape[:2]
    for tile in range(tiles // 2):
        place = core * (tiles // 2) + tile
        total[place] = partial[place]
    for load, (start, size) in zip(loads, chunks):
        load.wait()
        part = dot(attended[...], weight[:, start : start + size], ((1,), (0,)))
        for tile in range(size // LANES):
            place = (1 - core) * (tiles // 2) + start // LANES + tile
            total[place] = partial[place] + part[:, tile * LANES : (tile + 1) * LANES]
    values = jnp.concatenate([total[tile] for tile in range(tiles)], axis=1)
    normed = normalize(values)
    for tile in range(tiles):
        total[tile] = normed[:, tile * LANES : (tile + 1) * LANES]
    width = tiles * LANES
    projected = jnp.zeros(block.shape, jnp.float32)
    for quarter in range(4):
        part = [total[tile, pl.ds(quarter, rows // 4, stride=4), :] for tile in range(tiles)]
        part = jnp.concatenate(part, axis=1).astype(jnp.bfloat16)
        weight = merge_weight[:, quarter * width : (quarter + 1) * width]
        projected += dot(weight, part, ((1,), (1,)))
    block[...] = projected.astype(block.dtype)
    copies = [
        pltpu.make_async_copy(block, out.at[copy], sems.at[copy]) for copy in range(out.shape[0])
    ]
    for copy in copies:
        copy.start()
    for copy in copies:
        copy.wait()


def pick_kernel(wanted, blocks, out, sems):
    copies = [
        pltpu.make_async_copy(blocks.at[wanted[slot]], out.at[slot], sems.at[slot])
        for slot in range(out.shape[0])
    ]
    for copy in copies:
        copy.start()
    for copy in copies:
        copy.wait()


def deliver_kernel(facts, blocks, out):
    source = 2 * facts[0]
    pair = jnp.concatenate([blocks[source], blocks[source + 1]], axis=1)
    shape = (pair.shape[1], out.shape[1])
    row = lax.broadcasted_iota(jnp.int32, shape, 0) - facts[1]
    slot = lax.broadcasted_iota(jnp.int32, shape, 1)
    chosen = row == jnp.where(slot < facts[2], slot, -shape[0])
    chosen = jnp.where(chosen, 1.0, 0.0).astype(jnp.bfloat16)
    out[...] = dot(pair, chosen, ((1,), (0,))).astype(out.dtype)


def on_device(
    patches,
    row_table,
    col_table,
    qkv_weight,
    out_weight,
    merge_weight,
    segment_ids,
    image_grids,
    image_offsets,
    owners,
):
    block_rows, width = patches.shape
    width_here = qkv_weight.shape[1]
    group = lax.axis_size("head")
    places = lax.axis_size("tok")
    place = lax.axis_index("tok")
    params = pltpu.CompilerParams(vmem_limit_bytes=24 * 2**20)
    at_hbm = lambda x: pltpu.with_memory_space_constraint(x, pltpu.HBM)

    sides = places // (RING * 2)
    tok_of = [[[(x * RING + y) * 2 + c for c in range(2)] for y in range(RING)] for x in range(sides)]
    rings_y = [[tok_of[x][y][c] for y in range(RING)] for x in range(sides) for c in range(2)]
    rings_x = [[tok_of[x][y][c] for x in range(sides)] for y in range(RING) for c in range(2)]
    planes = [[tok_of[x][y][c] for x in range(sides) for c in range(2)] for y in range(RING)]
    my_x = place // (2 * RING)
    my_y = place // 2 % RING
    core = place % 2

    depth, columns = width_here // sides, width // 2
    piece = lax.dynamic_slice(out_weight, (my_x * depth, core * columns), (depth, columns))
    pieces = jnp.broadcast_to(piece[None], (group, depth, columns))
    pieces = lax.all_to_all(pieces, "head", 0, 0, tiled=True)

    resid, queries, near = pl.pallas_call(
        front_kernel,
        out_shape=(
            pltpu.HBM((width // LANES, block_rows, LANES), jnp.float32),
            jax.ShapeDtypeStruct((width_here, block_rows), jnp.bfloat16),
            jax.ShapeDtypeStruct((2 * width_here, block_rows), jnp.bfloat16),
        ),
        in_specs=[HBM, VMEM, HBM, HBM, HBM],
        out_specs=(HBM, VMEM, VMEM),
        scratch_shapes=[
            pltpu.VMEM((width // LANES, block_rows, LANES), jnp.float32),
            pltpu.VMEM((2 * row_table.shape[0], width), jnp.bfloat16),
            pltpu.VMEM(qkv_weight.shape, jnp.bfloat16),
            pltpu.SMEM(image_offsets.shape, jnp.int32),
            pltpu.SemaphoreType.DMA((5,)),
        ],
        compiler_params=params,
        cost_estimate=pl.CostEstimate(
            flops=3 * 2 * block_rows * width * width_here, bytes_accessed=8 * 2**20, transcendentals=0
        ),
    )(at_hbm(image_offsets), patches, *map(at_hbm, (row_table, col_table, qkv_weight)))
    far = partner(near, "tok", 0)
    mixed, stats = pl.pallas_call(
        near_kernel,
        out_shape=(
            jax.ShapeDtypeStruct((width_here, block_rows), jnp.float32),
            jax.ShapeDtypeStruct((2 * width_here // HEAD_DIM, block_rows), jnp.float32),
        ),
        in_specs=[SMEM, VMEM, VMEM],
        out_specs=(VMEM, VMEM),
        compiler_params=params,
        cost_estimate=pl.CostEstimate(
            flops=4 * block_rows * block_rows * width_here,
            bytes_accessed=2**21,
            transcendentals=block_rows * block_rows * 2,
        ),
    )(image_offsets, queries, near)
    sent = pl.pallas_call(
        far_kernel,
        out_shape=pltpu.HBM((group, width_here, block_rows), jnp.bfloat16),
        in_specs=[SMEM, VMEM, VMEM, VMEM, VMEM],
        out_specs=HBM,
        scratch_shapes=[
            pltpu.VMEM((width_here, block_rows), jnp.bfloat16),
            pltpu.SemaphoreType.DMA((width_here // HEAD_DIM, group)),
        ],
        compiler_params=params,
    )(image_offsets, queries, far, mixed, stats)
    pieces, sent = lax.optimization_barrier((pieces, sent))
    own_weight = lax.all_gather(pieces, "tok", axis=0, axis_index_groups=rings_x)
    own_weight = own_weight.transpose(1, 0, 2, 3).reshape(group * width_here, columns)
    other_weight = partner(own_weight, "tok", 0)

    gathered = lax.all_to_all(sent, "head", 0, 0, tiled=True)
    rows_here = block_rows // 4
    blocks_shape = pltpu.HBM((RING, width_here, rows_here), jnp.bfloat16)
    tiles = width // LANES
    half_flops = 2 * block_rows * width * columns
    attended, partial, merge_here = pl.pallas_call(
        project_kernel,
        out_shape=(
            jax.ShapeDtypeStruct((block_rows, width), jnp.bfloat16),
            jax.ShapeDtypeStruct((tiles, block_rows, LANES), jnp.float32),
            jax.ShapeDtypeStruct(merge_weight.shape, jnp.bfloat16),
        ),
        in_specs=[VMEM, VMEM, HBM, HBM],
        out_specs=(VMEM, VMEM, VMEM),
        scratch_shapes=[
            pltpu.VMEM((tiles, block_rows, LANES), jnp.float32),
            pltpu.SemaphoreType.DMA((2,)),
        ],
        compiler_params=params,
        cost_estimate=pl.CostEstimate(
            flops=half_flops, bytes_accessed=8 * 2**20, transcendentals=0
        ),
    )(gathered, own_weight, at_hbm(resid), at_hbm(merge_weight))
    projected = pl.pallas_call(
        merge_kernel,
        out_shape=blocks_shape,
        in_specs=[VMEM, HBM, VMEM, VMEM],
        out_specs=HBM,
        scratch_shapes=[
            pltpu.VMEM(other_weight.shape, jnp.bfloat16),
            pltpu.VMEM((tiles, block_rows, LANES), jnp.float32),
            pltpu.VMEM((width_here, rows_here), jnp.bfloat16),
            pltpu.SemaphoreType.DMA((columns // 256 + 1,)),
            pltpu.SemaphoreType.DMA((RING,)),
        ],
        compiler_params=params,
    )(attended, at_hbm(other_weight), partial, merge_here)

    image_ids = jnp.arange(owners.shape[0], dtype=jnp.int32)
    place_ids = jnp.arange(places, dtype=jnp.int32)
    image_of = jnp.sum(jnp.where(owners[None, :] == place_ids[:, None], image_ids[None, :], 0), axis=1)
    pair_y = (image_of // 2 % RING).reshape(sides, RING, 2)
    wanted = jnp.sum(
        jnp.where((jnp.arange(RING) == my_y)[None, :, None], pair_y, 0), axis=1
    ).reshape(2 * sides)
    mine = owners == place
    tokens = image_grids[:, 0] * image_grids[:, 1]
    first_token = image_offsets - image_ids // 2 * (2 * block_rows)
    facts = jnp.stack([image_ids // 2 // RING, first_token // 4, tokens // 4])
    facts = jnp.sum(jnp.where(mine[None, :], facts, 0), axis=1)

    blocks = lax.all_to_all(projected, "tok", 0, 0, axis_index_groups=rings_y, tiled=True)
    blocks = pl.pallas_call(
        pick_kernel,
        out_shape=pltpu.HBM((2 * sides, width_here, rows_here), jnp.bfloat16),
        in_specs=[SMEM, ANY],
        out_specs=HBM,
        scratch_shapes=[pltpu.SemaphoreType.DMA((2 * sides,))],
        compiler_params=params,
    )(wanted, blocks)
    blocks = lax.all_to_all(blocks, "tok", 0, 0, axis_index_groups=planes, tiled=True)
    return pl.pallas_call(
        deliver_kernel,
        out_shape=jax.ShapeDtypeStruct((width_here, CAP), jnp.bfloat16),
        in_specs=[SMEM, VMEM],
        out_specs=VMEM,
        compiler_params=params,
    )(facts, blocks).T


def solution(mesh):
    placed = (
        P("tok", None),
        P(),
        P(),
        P(None, "head", None),
        P("head", None),
        P("head", None),
        P("tok"),
        P(),
        P(),
        P(),
    )
    return jax.shard_map(
        on_device, mesh=mesh, in_specs=placed, out_specs=P("tok", "head"), check_vma=False
    )
```

```python
import math

import jax
import jax.numpy as jnp
from jax import lax
from jax.experimental import pallas as pl
from jax.experimental.pallas import tpu as pltpu
from jax.sharding import PartitionSpec as P

HEAD_DIM = 80
CAP = 248
WIDTH = 16
LANES = 128
RING = 8
SCALE = 1.0 / math.sqrt(HEAD_DIM)
MASKED = -1e30

VMEM = pl.BlockSpec(memory_space=pltpu.VMEM)
SMEM = pl.BlockSpec(memory_space=pltpu.SMEM)
HBM = pl.BlockSpec(memory_space=pltpu.HBM)
ANY = pl.BlockSpec(memory_space=pl.ANY)


def partner(x, axis, apart):
    return lax.ppermute(x, axis, [(i, i ^ 1 << apart) for i in range(lax.axis_size(axis))])


def normalize(values):
    centered = values - jnp.mean(values, axis=-1, keepdims=True)
    variance = jnp.mean(centered * centered, axis=-1, keepdims=True)
    return centered * lax.rsqrt(variance + 1e-06)


def dot(left, right, dims):
    return lax.dot_general(left, right, (dims, ((), ())), preferred_element_type=jnp.float32)


def front_kernel(
    offsets_hbm,
    patches,
    row_hbm,
    col_hbm,
    weight_hbm,
    resid_hbm,
    queries,
    pairs,
    resid,
    tables,
    weight,
    offsets,
    sems,
):
    rows = patches.shape[0]
    side = tables.shape[0] // 2
    copies = [
        pltpu.make_async_copy(row_hbm, tables.at[pl.ds(0, side), :], sems.at[0]),
        pltpu.make_async_copy(col_hbm, tables.at[pl.ds(side, side), :], sems.at[1]),
        pltpu.make_async_copy(weight_hbm, weight, sems.at[2]),
    ]
    offsets_copy = pltpu.make_async_copy(offsets_hbm, offsets, sems.at[4])
    offsets_copy.start()
    for copy in copies:
        copy.start()
    offsets_copy.wait()
    place = lax.axis_index("tok")
    first = place // 2 * 2
    position = place * rows + lax.broadcasted_iota(jnp.int32, (rows, 2 * side), 0)
    start = jnp.where(position >= offsets[first + 1], offsets[first + 1], offsets[first])
    local = position - start
    window = local >> 2
    quarter = local & 3
    half = WIDTH // 2
    row = 2 * (window // half) + (quarter >> 1)
    col = 2 * (window % half) + (quarter & 1)
    lane = lax.broadcasted_iota(jnp.int32, (rows, 2 * side), 1)
    onehot = lane == jnp.where(lane < side, row, col + side)
    onehot = jnp.where(onehot, 1.0, 0.0).astype(jnp.bfloat16)
    copies[0].wait()
    copies[1].wait()
    embedded = dot(onehot, tables[...], ((1,), (0,)))
    values = patches[...].astype(jnp.float32) + embedded
    for tile in range(resid.shape[0]):
        resid[tile] = values[:, tile * LANES : (tile + 1) * LANES]
    resid_copy = pltpu.make_async_copy(resid, resid_hbm, sems.at[3])
    resid_copy.start()
    normed = normalize(values).astype(jnp.bfloat16)
    copies[2].wait()
    width = weight.shape[1]
    wide = weight[...].reshape(3 * width, weight.shape[2])
    out = dot(wide, normed, ((1,), (1,))).astype(jnp.bfloat16)
    queries[...] = out[:width]
    pairs[...] = out[width:]
    resid_copy.wait()


def block_scores(offsets, block, query, other):
    rows = query.shape[1]
    place = lax.axis_index("tok")
    border = offsets[place // 2 * 2 + 1]
    key_place = jnp.where(place % 2 == 0, place + 1, place - 1) if other else place
    query_pos = place * rows + lax.broadcasted_iota(jnp.int32, (1, rows), 1)
    key_pos = key_place * rows + lax.broadcasted_iota(jnp.int32, (rows, 1), 0)
    query_side = jnp.where(query_pos >= border, 1, 0)
    key_side = jnp.where(key_pos >= border, 1, 0)
    scores = dot(block, query, ((0,), (0,))) * SCALE
    return jnp.where(key_side == query_side, scores, MASKED)


def near_kernel(offsets, queries, near, mixed, stats):
    width = queries.shape[0]
    for head in range(width // HEAD_DIM):
        own = slice(head * HEAD_DIM, (head + 1) * HEAD_DIM)
        value = slice(width + head * HEAD_DIM, width + (head + 1) * HEAD_DIM)
        scores = block_scores(offsets, near[own, :], queries[own, :], False)
        top = jnp.max(scores, axis=0, keepdims=True)
        expo = jnp.exp(scores - top)
        stats[2 * head : 2 * head + 1, :] = top
        stats[2 * head + 1 : 2 * head + 2, :] = jnp.sum(expo, axis=0, keepdims=True)
        mixed[own, :] = dot(near[value, :], expo.astype(jnp.bfloat16), ((1,), (0,)))


def far_kernel(offsets, queries, far, near_mixed, stats, out, attended, sems):
    width = queries.shape[0]
    copies = []
    for head in range(width // HEAD_DIM):
        own = slice(head * HEAD_DIM, (head + 1) * HEAD_DIM)
        value = slice(width + head * HEAD_DIM, width + (head + 1) * HEAD_DIM)
        scores = block_scores(offsets, far[own, :], queries[own, :], True)
        near_top = stats[2 * head : 2 * head + 1, :]
        top = jnp.maximum(near_top, jnp.max(scores, axis=0, keepdims=True))
        expo = jnp.exp(scores - top)
        scale = jnp.exp(near_top - top)
        total = stats[2 * head + 1 : 2 * head + 2, :] * scale
        total += jnp.sum(expo, axis=0, keepdims=True)
        mixed = near_mixed[own, :] * scale
        mixed += dot(far[value, :], expo.astype(jnp.bfloat16), ((1,), (0,)))
        attended[own, :] = (mixed / total).astype(jnp.bfloat16)
        part = pl.ds(head * HEAD_DIM, HEAD_DIM)
        for copy in range(out.shape[0]):
            copies.append(
                pltpu.make_async_copy(
                    attended.at[part, :], out.at[copy, part, :], sems.at[head, copy]
                )
            )
            copies[-1].start()
    for copy in copies:
        copy.wait()


def project_kernel(
    gathered, weight, resid_hbm, merge_hbm, attended, partial, merge_weight, resid, sems
):
    resid_copy = pltpu.make_async_copy(resid_hbm, resid, sems.at[0])
    resid_copy.start()
    merge_copy = pltpu.make_async_copy(merge_hbm, merge_weight, sems.at[1])
    merge_copy.start()
    core = lax.axis_index("tok") % 2
    group, depth, rows = gathered.shape
    whole = gathered[...].reshape(group * depth, rows)
    tiles = resid.shape[0]
    for tile in range(tiles):
        part = slice(tile * LANES, (tile + 1) * LANES)
        attended[:, part] = whole[part, :].T
    part = dot(attended[...], weight[...], ((1,), (0,)))
    resid_copy.wait()
    for tile in range(tiles // 2):
        place = core * (tiles // 2) + tile
        partial[place] = resid[place] + part[:, tile * LANES : (tile + 1) * LANES]
        place = (1 - core) * (tiles // 2) + tile
        partial[place] = resid[place]
    merge_copy.wait()


def merge_kernel(
    attended, weight_hbm, partial, merge_weight, out, weight, total, block, weight_sems, sems
):
    chunks = [(start, min(256, weight.shape[1] - start)) for start in range(0, weight.shape[1], 256)]
    loads = [
        pltpu.make_async_copy(
            weight_hbm.at[:, pl.ds(start, size)],
            weight.at[:, pl.ds(start, size)],
            weight_sems.at[chunk],
        )
        for chunk, (start, size) in enumerate(chunks)
    ]
    for load in loads:
        load.start()
    core = lax.axis_index("tok") % 2
    tiles, rows = partial.shape[:2]
    for tile in range(tiles // 2):
        place = core * (tiles // 2) + tile
        total[place] = partial[place]
    for load, (start, size) in zip(loads, chunks):
        load.wait()
        part = dot(attended[...], weight[:, start : start + size], ((1,), (0,)))
        for tile in range(size // LANES):
            place = (1 - core) * (tiles // 2) + start // LANES + tile
            total[place] = partial[place] + part[:, tile * LANES : (tile + 1) * LANES]
    values = jnp.concatenate([total[tile] for tile in range(tiles)], axis=1)
    normed = normalize(values)
    for tile in range(tiles):
        total[tile] = normed[:, tile * LANES : (tile + 1) * LANES]
    width = tiles * LANES
    projected = jnp.zeros(block.shape, jnp.float32)
    for quarter in range(4):
        part = [total[tile, pl.ds(quarter, rows // 4, stride=4), :] for tile in range(tiles)]
        part = jnp.concatenate(part, axis=1).astype(jnp.bfloat16)
        weight = merge_weight[:, quarter * width : (quarter + 1) * width]
        projected += dot(weight, part, ((1,), (1,)))
    block[...] = projected.astype(block.dtype)
    copies = [
        pltpu.make_async_copy(block, out.at[copy], sems.at[copy]) for copy in range(out.shape[0])
    ]
    for copy in copies:
        copy.start()
    for copy in copies:
        copy.wait()


def pick_kernel(wanted, blocks, out, sems):
    copies = [
        pltpu.make_async_copy(blocks.at[wanted[slot]], out.at[slot], sems.at[slot])
        for slot in range(out.shape[0])
    ]
    for copy in copies:
        copy.start()
    for copy in copies:
        copy.wait()


def deliver_kernel(facts, blocks, out):
    source = 2 * facts[0]
    pair = jnp.concatenate([blocks[source], blocks[source + 1]], axis=1)
    shape = (pair.shape[1], out.shape[1])
    row = lax.broadcasted_iota(jnp.int32, shape, 0) - facts[1]
    slot = lax.broadcasted_iota(jnp.int32, shape, 1)
    chosen = row == jnp.where(slot < facts[2], slot, -shape[0])
    chosen = jnp.where(chosen, 1.0, 0.0).astype(jnp.bfloat16)
    out[...] = dot(pair, chosen, ((1,), (0,))).astype(out.dtype)


def on_device(
    patches,
    row_table,
    col_table,
    qkv_weight,
    out_weight,
    merge_weight,
    segment_ids,
    image_grids,
    image_offsets,
    owners,
):
    block_rows, width = patches.shape
    width_here = qkv_weight.shape[1]
    group = lax.axis_size("head")
    places = lax.axis_size("tok")
    place = lax.axis_index("tok")
    params = pltpu.CompilerParams(vmem_limit_bytes=24 * 2**20)
    at_hbm = lambda x: pltpu.with_memory_space_constraint(x, pltpu.HBM)

    sides = places // (RING * 2)
    tok_of = [[[(x * RING + y) * 2 + c for c in range(2)] for y in range(RING)] for x in range(sides)]
    rings_y = [[tok_of[x][y][c] for y in range(RING)] for x in range(sides) for c in range(2)]
    rings_x = [[tok_of[x][y][c] for x in range(sides)] for y in range(RING) for c in range(2)]
    planes = [[tok_of[x][y][c] for x in range(sides) for c in range(2)] for y in range(RING)]
    my_x = place // (2 * RING)
    my_y = place // 2 % RING
    core = place % 2

    depth, columns = width_here // sides, width // 2
    piece = lax.dynamic_slice(out_weight, (my_x * depth, core * columns), (depth, columns))
    pieces = jnp.broadcast_to(piece[None], (group, depth, columns))
    pieces = lax.all_to_all(pieces, "head", 0, 0, tiled=True)

    resid, queries, near = pl.pallas_call(
        front_kernel,
        out_shape=(
            pltpu.HBM((width // LANES, block_rows, LANES), jnp.float32),
            jax.ShapeDtypeStruct((width_here, block_rows), jnp.bfloat16),
            jax.ShapeDtypeStruct((2 * width_here, block_rows), jnp.bfloat16),
        ),
        in_specs=[HBM, VMEM, HBM, HBM, HBM],
        out_specs=(HBM, VMEM, VMEM),
        scratch_shapes=[
            pltpu.VMEM((width // LANES, block_rows, LANES), jnp.float32),
            pltpu.VMEM((2 * row_table.shape[0], width), jnp.bfloat16),
            pltpu.VMEM(qkv_weight.shape, jnp.bfloat16),
            pltpu.SMEM(image_offsets.shape, jnp.int32),
            pltpu.SemaphoreType.DMA((5,)),
        ],
        compiler_params=params,
        cost_estimate=pl.CostEstimate(
            flops=3 * 2 * block_rows * width * width_here, bytes_accessed=8 * 2**20, transcendentals=0
        ),
    )(at_hbm(image_offsets), patches, *map(at_hbm, (row_table, col_table, qkv_weight)))
    far = partner(near, "tok", 0)
    mixed, stats = pl.pallas_call(
        near_kernel,
        out_shape=(
            jax.ShapeDtypeStruct((width_here, block_rows), jnp.float32),
            jax.ShapeDtypeStruct((2 * width_here // HEAD_DIM, block_rows), jnp.float32),
        ),
        in_specs=[SMEM, VMEM, VMEM],
        out_specs=(VMEM, VMEM),
        compiler_params=params,
        cost_estimate=pl.CostEstimate(
            flops=4 * block_rows * block_rows * width_here,
            bytes_accessed=2**21,
            transcendentals=block_rows * block_rows * 2,
        ),
    )(image_offsets, queries, near)
    sent = pl.pallas_call(
        far_kernel,
        out_shape=pltpu.HBM((group, width_here, block_rows), jnp.bfloat16),
        in_specs=[SMEM, VMEM, VMEM, VMEM, VMEM],
        out_specs=HBM,
        scratch_shapes=[
            pltpu.VMEM((width_here, block_rows), jnp.bfloat16),
            pltpu.SemaphoreType.DMA((width_here // HEAD_DIM, group)),
        ],
        compiler_params=params,
    )(image_offsets, queries, far, mixed, stats)
    pieces, sent = lax.optimization_barrier((pieces, sent))
    own_weight = [
        lax.all_gather(part, "tok", axis=0, axis_index_groups=rings_x)
        for part in jnp.split(pieces, 2)
    ]
    own_weight = jnp.concatenate([part.transpose(1, 0, 2, 3) for part in own_weight], axis=0)
    own_weight = own_weight.reshape(group * width_here, columns)
    other_weight = partner(own_weight, "tok", 0)

    gathered = lax.all_to_all(sent, "head", 0, 0, tiled=True)
    rows_here = block_rows // 4
    blocks_shape = pltpu.HBM((RING, width_here, rows_here), jnp.bfloat16)
    tiles = width // LANES
    half_flops = 2 * block_rows * width * columns
    attended, partial, merge_here = pl.pallas_call(
        project_kernel,
        out_shape=(
            jax.ShapeDtypeStruct((block_rows, width), jnp.bfloat16),
            jax.ShapeDtypeStruct((tiles, block_rows, LANES), jnp.float32),
            jax.ShapeDtypeStruct(merge_weight.shape, jnp.bfloat16),
        ),
        in_specs=[VMEM, VMEM, HBM, HBM],
        out_specs=(VMEM, VMEM, VMEM),
        scratch_shapes=[
            pltpu.VMEM((tiles, block_rows, LANES), jnp.float32),
            pltpu.SemaphoreType.DMA((2,)),
        ],
        compiler_params=params,
        cost_estimate=pl.CostEstimate(
            flops=half_flops, bytes_accessed=8 * 2**20, transcendentals=0
        ),
    )(gathered, own_weight, at_hbm(resid), at_hbm(merge_weight))
    projected = pl.pallas_call(
        merge_kernel,
        out_shape=blocks_shape,
        in_specs=[VMEM, HBM, VMEM, VMEM],
        out_specs=HBM,
        scratch_shapes=[
            pltpu.VMEM(other_weight.shape, jnp.bfloat16),
            pltpu.VMEM((tiles, block_rows, LANES), jnp.float32),
            pltpu.VMEM((width_here, rows_here), jnp.bfloat16),
            pltpu.SemaphoreType.DMA((columns // 256 + 1,)),
            pltpu.SemaphoreType.DMA((RING,)),
        ],
        compiler_params=params,
    )(attended, at_hbm(other_weight), partial, merge_here)

    image_ids = jnp.arange(owners.shape[0], dtype=jnp.int32)
    place_ids = jnp.arange(places, dtype=jnp.int32)
    image_of = jnp.sum(jnp.where(owners[None, :] == place_ids[:, None], image_ids[None, :], 0), axis=1)
    pair_y = (image_of // 2 % RING).reshape(sides, RING, 2)
    wanted = jnp.sum(
        jnp.where((jnp.arange(RING) == my_y)[None, :, None], pair_y, 0), axis=1
    ).reshape(2 * sides)
    mine = owners == place
    tokens = image_grids[:, 0] * image_grids[:, 1]
    first_token = image_offsets - image_ids // 2 * (2 * block_rows)
    facts = jnp.stack([image_ids // 2 // RING, first_token // 4, tokens // 4])
    facts = jnp.sum(jnp.where(mine[None, :], facts, 0), axis=1)

    blocks = lax.all_to_all(projected, "tok", 0, 0, axis_index_groups=rings_y, tiled=True)
    blocks = pl.pallas_call(
        pick_kernel,
        out_shape=pltpu.HBM((2 * sides, width_here, rows_here), jnp.bfloat16),
        in_specs=[SMEM, ANY],
        out_specs=HBM,
        scratch_shapes=[pltpu.SemaphoreType.DMA((2 * sides,))],
        compiler_params=params,
    )(wanted, blocks)
    blocks = lax.all_to_all(blocks, "tok", 0, 0, axis_index_groups=planes, tiled=True)
    return pl.pallas_call(
        deliver_kernel,
        out_shape=jax.ShapeDtypeStruct((width_here, CAP), jnp.bfloat16),
        in_specs=[SMEM, VMEM],
        out_specs=VMEM,
        compiler_params=params,
    )(facts, blocks).T


def solution(mesh):
    placed = (
        P("tok", None),
        P(),
        P(),
        P(None, "head", None),
        P("head", None),
        P("head", None),
        P("tok"),
        P(),
        P(),
        P(),
    )
    return jax.shard_map(
        on_device, mesh=mesh, in_specs=placed, out_specs=P("tok", "head"), check_vma=False
    )
```

```python
import math

import jax
import jax.numpy as jnp
from jax import lax
from jax.experimental import pallas as pl
from jax.experimental.pallas import tpu as pltpu
from jax.sharding import PartitionSpec as P

HEAD_DIM = 80
CAP = 248
WIDTH = 16
LANES = 128
RING = 8
SCALE = 1.0 / math.sqrt(HEAD_DIM)
MASKED = -1e30

VMEM = pl.BlockSpec(memory_space=pltpu.VMEM)
SMEM = pl.BlockSpec(memory_space=pltpu.SMEM)
HBM = pl.BlockSpec(memory_space=pltpu.HBM)
ANY = pl.BlockSpec(memory_space=pl.ANY)


def partner(x, axis, apart):
    return lax.ppermute(x, axis, [(i, i ^ 1 << apart) for i in range(lax.axis_size(axis))])


def normalize(values):
    centered = values - jnp.mean(values, axis=-1, keepdims=True)
    variance = jnp.mean(centered * centered, axis=-1, keepdims=True)
    return centered * lax.rsqrt(variance + 1e-06)


def dot(left, right, dims):
    return lax.dot_general(left, right, (dims, ((), ())), preferred_element_type=jnp.float32)


def front_kernel(
    offsets_hbm,
    patches,
    row_hbm,
    col_hbm,
    weight_hbm,
    resid_hbm,
    queries,
    pairs,
    resid,
    tables,
    weight,
    offsets,
    sems,
    weight_sems,
    resid_sems,
):
    rows = patches.shape[0]
    side = tables.shape[0] // 2
    copies = [
        pltpu.make_async_copy(row_hbm, tables.at[pl.ds(0, side), :], sems.at[0]),
        pltpu.make_async_copy(col_hbm, tables.at[pl.ds(side, side), :], sems.at[1]),
    ]
    weight_copies = [
        pltpu.make_async_copy(weight_hbm.at[part], weight.at[part], weight_sems.at[part])
        for part in range(weight.shape[0])
    ]
    offsets_copy = pltpu.make_async_copy(offsets_hbm, offsets, sems.at[2])
    offsets_copy.start()
    for copy in copies + weight_copies:
        copy.start()
    offsets_copy.wait()
    place = lax.axis_index("tok")
    first = place // 2 * 2
    position = place * rows + lax.broadcasted_iota(jnp.int32, (rows, 2 * side), 0)
    start = jnp.where(position >= offsets[first + 1], offsets[first + 1], offsets[first])
    local = position - start
    window = local >> 2
    quarter = local & 3
    half = WIDTH // 2
    row = 2 * (window // half) + (quarter >> 1)
    col = 2 * (window % half) + (quarter & 1)
    lane = lax.broadcasted_iota(jnp.int32, (rows, 2 * side), 1)
    onehot = lane == jnp.where(lane < side, row, col + side)
    onehot = jnp.where(onehot, 1.0, 0.0).astype(jnp.bfloat16)
    copies[0].wait()
    copies[1].wait()
    embedded = dot(onehot, tables[...], ((1,), (0,)))
    values = patches[...].astype(jnp.float32) + embedded
    resid_copies = []
    for tile in range(resid.shape[0]):
        resid[tile] = values[:, tile * LANES : (tile + 1) * LANES]
        resid_copies.append(
            pltpu.make_async_copy(resid.at[tile], resid_hbm.at[tile], resid_sems.at[tile])
        )
        resid_copies[-1].start()
    normed = normalize(values).astype(jnp.bfloat16)
    for copy in weight_copies:
        copy.wait()
    width = weight.shape[1]
    wide = weight[...].reshape(3 * width, weight.shape[2])
    out = dot(wide, normed, ((1,), (1,))).astype(jnp.bfloat16)
    queries[...] = out[:width]
    pairs[...] = out[width:]
    for copy in resid_copies:
        copy.wait()


def block_scores(offsets, block, query, other):
    rows = query.shape[1]
    place = lax.axis_index("tok")
    border = offsets[place // 2 * 2 + 1]
    key_place = jnp.where(place % 2 == 0, place + 1, place - 1) if other else place
    query_pos = place * rows + lax.broadcasted_iota(jnp.int32, (1, rows), 1)
    key_pos = key_place * rows + lax.broadcasted_iota(jnp.int32, (rows, 1), 0)
    query_side = jnp.where(query_pos >= border, 1, 0)
    key_side = jnp.where(key_pos >= border, 1, 0)
    scores = dot(block, query, ((0,), (0,))) * SCALE
    return jnp.where(key_side == query_side, scores, MASKED)


def near_kernel(offsets, queries, near, mixed, stats):
    width = queries.shape[0]
    for head in range(width // HEAD_DIM):
        own = slice(head * HEAD_DIM, (head + 1) * HEAD_DIM)
        value = slice(width + head * HEAD_DIM, width + (head + 1) * HEAD_DIM)
        scores = block_scores(offsets, near[own, :], queries[own, :], False)
        top = jnp.max(scores, axis=0, keepdims=True)
        expo = jnp.exp(scores - top)
        stats[2 * head : 2 * head + 1, :] = top
        stats[2 * head + 1 : 2 * head + 2, :] = jnp.sum(expo, axis=0, keepdims=True)
        mixed[own, :] = dot(near[value, :], expo.astype(jnp.bfloat16), ((1,), (0,)))


def far_kernel(offsets, queries, far, near_mixed, stats, out, attended, sems):
    width = queries.shape[0]
    copies = []
    for head in range(width // HEAD_DIM):
        own = slice(head * HEAD_DIM, (head + 1) * HEAD_DIM)
        value = slice(width + head * HEAD_DIM, width + (head + 1) * HEAD_DIM)
        scores = block_scores(offsets, far[own, :], queries[own, :], True)
        near_top = stats[2 * head : 2 * head + 1, :]
        top = jnp.maximum(near_top, jnp.max(scores, axis=0, keepdims=True))
        expo = jnp.exp(scores - top)
        scale = jnp.exp(near_top - top)
        total = stats[2 * head + 1 : 2 * head + 2, :] * scale
        total += jnp.sum(expo, axis=0, keepdims=True)
        mixed = near_mixed[own, :] * scale
        mixed += dot(far[value, :], expo.astype(jnp.bfloat16), ((1,), (0,)))
        attended[own, :] = (mixed / total).astype(jnp.bfloat16)
        part = pl.ds(head * HEAD_DIM, HEAD_DIM)
        for copy in range(out.shape[0]):
            copies.append(
                pltpu.make_async_copy(
                    attended.at[part, :], out.at[copy, part, :], sems.at[head, copy]
                )
            )
            copies[-1].start()
    for copy in copies:
        copy.wait()


def project_kernel(
    gathered,
    weight,
    resid_hbm,
    merge_hbm,
    attended,
    partial,
    merge_weight,
    resid,
    resid_sems,
    merge_sems,
):
    resid_copies = [
        pltpu.make_async_copy(resid_hbm.at[tile], resid.at[tile], resid_sems.at[tile])
        for tile in range(resid.shape[0])
    ]
    depth = merge_weight.shape[0] // 4
    merge_copies = [
        pltpu.make_async_copy(
            merge_hbm.at[pl.ds(i * depth, depth), :],
            merge_weight.at[pl.ds(i * depth, depth), :],
            merge_sems.at[i],
        )
        for i in range(4)
    ]
    for copy in resid_copies + merge_copies:
        copy.start()
    core = lax.axis_index("tok") % 2
    group, depth, rows = gathered.shape
    whole = gathered[...].reshape(group * depth, rows)
    tiles = resid.shape[0]
    for tile in range(tiles):
        part = slice(tile * LANES, (tile + 1) * LANES)
        attended[:, part] = whole[part, :].T
    part = dot(attended[...], weight[...], ((1,), (0,)))
    for copy in resid_copies:
        copy.wait()
    for tile in range(tiles // 2):
        place = core * (tiles // 2) + tile
        partial[place] = resid[place] + part[:, tile * LANES : (tile + 1) * LANES]
        place = (1 - core) * (tiles // 2) + tile
        partial[place] = resid[place]
    for copy in merge_copies:
        copy.wait()


def merge_kernel(
    attended, weight_hbm, partial, merge_weight, out, weight, total, block, weight_sems, sems
):
    chunks = [(start, min(256, weight.shape[1] - start)) for start in range(0, weight.shape[1], 256)]
    loads = [
        pltpu.make_async_copy(
            weight_hbm.at[:, pl.ds(start, size)],
            weight.at[:, pl.ds(start, size)],
            weight_sems.at[chunk],
        )
        for chunk, (start, size) in enumerate(chunks)
    ]
    for load in loads:
        load.start()
    core = lax.axis_index("tok") % 2
    tiles, rows = partial.shape[:2]
    for tile in range(tiles // 2):
        place = core * (tiles // 2) + tile
        total[place] = partial[place]
    for load, (start, size) in zip(loads, chunks):
        load.wait()
        part = dot(attended[...], weight[:, start : start + size], ((1,), (0,)))
        for tile in range(size // LANES):
            place = (1 - core) * (tiles // 2) + start // LANES + tile
            total[place] = partial[place] + part[:, tile * LANES : (tile + 1) * LANES]
    values = jnp.concatenate([total[tile] for tile in range(tiles)], axis=1)
    normed = normalize(values)
    for tile in range(tiles):
        total[tile] = normed[:, tile * LANES : (tile + 1) * LANES]
    width = tiles * LANES
    projected = jnp.zeros(block.shape, jnp.float32)
    for quarter in range(4):
        part = [total[tile, pl.ds(quarter, rows // 4, stride=4), :] for tile in range(tiles)]
        part = jnp.concatenate(part, axis=1).astype(jnp.bfloat16)
        weight = merge_weight[:, quarter * width : (quarter + 1) * width]
        projected += dot(weight, part, ((1,), (1,)))
    block[...] = projected.astype(block.dtype)
    copies = [
        pltpu.make_async_copy(block, out.at[copy], sems.at[copy]) for copy in range(out.shape[0])
    ]
    for copy in copies:
        copy.start()
    for copy in copies:
        copy.wait()


def pick_kernel(wanted, blocks, out, sems):
    copies = [
        pltpu.make_async_copy(blocks.at[wanted[slot]], out.at[slot], sems.at[slot])
        for slot in range(out.shape[0])
    ]
    for copy in copies:
        copy.start()
    for copy in copies:
        copy.wait()


def deliver_kernel(facts, blocks, out):
    source = 2 * facts[0]
    pair = jnp.concatenate([blocks[source], blocks[source + 1]], axis=1)
    shape = (pair.shape[1], out.shape[1])
    row = lax.broadcasted_iota(jnp.int32, shape, 0) - facts[1]
    slot = lax.broadcasted_iota(jnp.int32, shape, 1)
    chosen = row == jnp.where(slot < facts[2], slot, -shape[0])
    chosen = jnp.where(chosen, 1.0, 0.0).astype(jnp.bfloat16)
    out[...] = dot(pair, chosen, ((1,), (0,))).astype(out.dtype)


def on_device(
    patches,
    row_table,
    col_table,
    qkv_weight,
    out_weight,
    merge_weight,
    segment_ids,
    image_grids,
    image_offsets,
    owners,
):
    block_rows, width = patches.shape
    width_here = qkv_weight.shape[1]
    group = lax.axis_size("head")
    places = lax.axis_size("tok")
    place = lax.axis_index("tok")
    params = pltpu.CompilerParams(vmem_limit_bytes=24 * 2**20)
    at_hbm = lambda x: pltpu.with_memory_space_constraint(x, pltpu.HBM)

    sides = places // (RING * 2)
    tok_of = [[[(x * RING + y) * 2 + c for c in range(2)] for y in range(RING)] for x in range(sides)]
    rings_y = [[tok_of[x][y][c] for y in range(RING)] for x in range(sides) for c in range(2)]
    rings_x = [[tok_of[x][y][c] for x in range(sides)] for y in range(RING) for c in range(2)]
    planes = [[tok_of[x][y][c] for x in range(sides) for c in range(2)] for y in range(RING)]
    my_x = place // (2 * RING)
    my_y = place // 2 % RING
    core = place % 2

    depth, columns = width_here // sides, width // 2
    piece = lax.dynamic_slice(out_weight, (my_x * depth, core * columns), (depth, columns))
    pieces = jnp.broadcast_to(piece[None], (group, depth, columns))
    pieces = lax.all_to_all(pieces, "head", 0, 0, tiled=True)

    resid, queries, near = pl.pallas_call(
        front_kernel,
        out_shape=(
            pltpu.HBM((width // LANES, block_rows, LANES), jnp.float32),
            jax.ShapeDtypeStruct((width_here, block_rows), jnp.bfloat16),
            jax.ShapeDtypeStruct((2 * width_here, block_rows), jnp.bfloat16),
        ),
        in_specs=[HBM, VMEM, HBM, HBM, HBM],
        out_specs=(HBM, VMEM, VMEM),
        scratch_shapes=[
            pltpu.VMEM((width // LANES, block_rows, LANES), jnp.float32),
            pltpu.VMEM((2 * row_table.shape[0], width), jnp.bfloat16),
            pltpu.VMEM(qkv_weight.shape, jnp.bfloat16),
            pltpu.SMEM(image_offsets.shape, jnp.int32),
            pltpu.SemaphoreType.DMA((3,)),
            pltpu.SemaphoreType.DMA((qkv_weight.shape[0],)),
            pltpu.SemaphoreType.DMA((width // LANES,)),
        ],
        compiler_params=params,
        cost_estimate=pl.CostEstimate(
            flops=3 * 2 * block_rows * width * width_here, bytes_accessed=8 * 2**20, transcendentals=0
        ),
    )(at_hbm(image_offsets), patches, *map(at_hbm, (row_table, col_table, qkv_weight)))
    far = partner(near, "tok", 0)
    mixed, stats = pl.pallas_call(
        near_kernel,
        out_shape=(
            jax.ShapeDtypeStruct((width_here, block_rows), jnp.float32),
            jax.ShapeDtypeStruct((2 * width_here // HEAD_DIM, block_rows), jnp.float32),
        ),
        in_specs=[SMEM, VMEM, VMEM],
        out_specs=(VMEM, VMEM),
        compiler_params=params,
        cost_estimate=pl.CostEstimate(
            flops=4 * block_rows * block_rows * width_here,
            bytes_accessed=2**21,
            transcendentals=block_rows * block_rows * 2,
        ),
    )(image_offsets, queries, near)
    sent = pl.pallas_call(
        far_kernel,
        out_shape=pltpu.HBM((group, width_here, block_rows), jnp.bfloat16),
        in_specs=[SMEM, VMEM, VMEM, VMEM, VMEM],
        out_specs=HBM,
        scratch_shapes=[
            pltpu.VMEM((width_here, block_rows), jnp.bfloat16),
            pltpu.SemaphoreType.DMA((width_here // HEAD_DIM, group)),
        ],
        compiler_params=params,
    )(image_offsets, queries, far, mixed, stats)
    pieces, sent = lax.optimization_barrier((pieces, sent))
    own_weight = [
        lax.all_gather(part, "tok", axis=1, axis_index_groups=rings_x, tiled=True)
        for part in jnp.split(pieces, 2)
    ]
    own_weight = jnp.concatenate(own_weight, axis=0).reshape(group * width_here, columns)
    other_weight = partner(own_weight, "tok", 0)

    gathered = lax.all_to_all(sent, "head", 0, 0, tiled=True)
    rows_here = block_rows // 4
    blocks_shape = pltpu.HBM((RING, width_here, rows_here), jnp.bfloat16)
    tiles = width // LANES
    half_flops = 2 * block_rows * width * columns
    attended, partial, merge_here = pl.pallas_call(
        project_kernel,
        out_shape=(
            jax.ShapeDtypeStruct((block_rows, width), jnp.bfloat16),
            jax.ShapeDtypeStruct((tiles, block_rows, LANES), jnp.float32),
            jax.ShapeDtypeStruct(merge_weight.shape, jnp.bfloat16),
        ),
        in_specs=[VMEM, VMEM, HBM, HBM],
        out_specs=(VMEM, VMEM, VMEM),
        scratch_shapes=[
            pltpu.VMEM((tiles, block_rows, LANES), jnp.float32),
            pltpu.SemaphoreType.DMA((tiles,)),
            pltpu.SemaphoreType.DMA((4,)),
        ],
        compiler_params=params,
        cost_estimate=pl.CostEstimate(
            flops=half_flops, bytes_accessed=8 * 2**20, transcendentals=0
        ),
    )(gathered, own_weight, at_hbm(resid), at_hbm(merge_weight))
    projected = pl.pallas_call(
        merge_kernel,
        out_shape=blocks_shape,
        in_specs=[VMEM, HBM, VMEM, VMEM],
        out_specs=HBM,
        scratch_shapes=[
            pltpu.VMEM(other_weight.shape, jnp.bfloat16),
            pltpu.VMEM((tiles, block_rows, LANES), jnp.float32),
            pltpu.VMEM((width_here, rows_here), jnp.bfloat16),
            pltpu.SemaphoreType.DMA((columns // 256 + 1,)),
            pltpu.SemaphoreType.DMA((RING,)),
        ],
        compiler_params=params,
    )(attended, at_hbm(other_weight), partial, merge_here)

    image_ids = jnp.arange(owners.shape[0], dtype=jnp.int32)
    place_ids = jnp.arange(places, dtype=jnp.int32)
    image_of = jnp.sum(jnp.where(owners[None, :] == place_ids[:, None], image_ids[None, :], 0), axis=1)
    pair_y = (image_of // 2 % RING).reshape(sides, RING, 2)
    wanted = jnp.sum(
        jnp.where((jnp.arange(RING) == my_y)[None, :, None], pair_y, 0), axis=1
    ).reshape(2 * sides)
    mine = owners == place
    tokens = image_grids[:, 0] * image_grids[:, 1]
    first_token = image_offsets - image_ids // 2 * (2 * block_rows)
    facts = jnp.stack([image_ids // 2 // RING, first_token // 4, tokens // 4])
    facts = jnp.sum(jnp.where(mine[None, :], facts, 0), axis=1)

    blocks = lax.all_to_all(projected, "tok", 0, 0, axis_index_groups=rings_y, tiled=True)
    blocks = pl.pallas_call(
        pick_kernel,
        out_shape=pltpu.HBM((2 * sides, width_here, rows_here), jnp.bfloat16),
        in_specs=[SMEM, ANY],
        out_specs=HBM,
        scratch_shapes=[pltpu.SemaphoreType.DMA((2 * sides,))],
        compiler_params=params,
    )(wanted, blocks)
    blocks = lax.all_to_all(blocks, "tok", 0, 0, axis_index_groups=planes, tiled=True)
    return pl.pallas_call(
        deliver_kernel,
        out_shape=jax.ShapeDtypeStruct((width_here, CAP), jnp.bfloat16),
        in_specs=[SMEM, VMEM],
        out_specs=VMEM,
        compiler_params=params,
    )(facts, blocks).T


def solution(mesh):
    placed = (
        P("tok", None),
        P(),
        P(),
        P(None, "head", None),
        P("head", None),
        P("head", None),
        P("tok"),
        P(),
        P(),
        P(),
    )
    return jax.shard_map(
        on_device, mesh=mesh, in_specs=placed, out_specs=P("tok", "head"), check_vma=False
    )
```

```python
import math

import jax
import jax.numpy as jnp
from jax import lax
from jax.experimental import pallas as pl
from jax.experimental.pallas import tpu as pltpu
from jax.sharding import PartitionSpec as P

HEAD_DIM = 80
CAP = 248
WIDTH = 16
LANES = 128
RING = 8
SCALE = 1.0 / math.sqrt(HEAD_DIM)
MASKED = -1e30

VMEM = pl.BlockSpec(memory_space=pltpu.VMEM)
SMEM = pl.BlockSpec(memory_space=pltpu.SMEM)
HBM = pl.BlockSpec(memory_space=pltpu.HBM)
ANY = pl.BlockSpec(memory_space=pl.ANY)


def partner(x, axis, apart):
    return lax.ppermute(x, axis, [(i, i ^ 1 << apart) for i in range(lax.axis_size(axis))])


def normalize(values):
    centered = values - jnp.mean(values, axis=-1, keepdims=True)
    variance = jnp.mean(centered * centered, axis=-1, keepdims=True)
    return centered * lax.rsqrt(variance + 1e-06)


def dot(left, right, dims):
    return lax.dot_general(left, right, (dims, ((), ())), preferred_element_type=jnp.float32)


def load_kernel(
    out_weight,
    row_hbm,
    col_hbm,
    qkv_hbm,
    offsets_hbm,
    pieces,
    tables,
    qkv_weight,
    onehot,
    piece,
    offsets,
    sems,
    piece_sems,
):
    depth, columns = piece.shape
    side = row_hbm.shape[0]
    place = lax.axis_index("tok")
    row = pl.multiple_of(place // (2 * RING) * depth, 8)
    column = pl.multiple_of(place % 2 * columns, LANES)
    first = pltpu.make_async_copy(
        out_weight.at[pl.ds(row, depth), pl.ds(column, columns)], piece, sems.at[0]
    )
    first.start()
    offsets_copy = pltpu.make_async_copy(offsets_hbm, offsets, piece_sems.at[pieces.shape[0]])
    offsets_copy.start()
    loads = [
        pltpu.make_async_copy(row_hbm, tables.at[pl.ds(0, side), :], sems.at[1]),
        pltpu.make_async_copy(col_hbm, tables.at[pl.ds(side, side), :], sems.at[2]),
    ]
    for part in range(qkv_hbm.shape[0]):
        loads.append(
            pltpu.make_async_copy(qkv_hbm.at[part], qkv_weight.at[part], sems.at[3 + part])
        )
    for load in loads:
        load.start()
    first.wait()
    copies = [
        pltpu.make_async_copy(piece, pieces.at[copy], piece_sems.at[copy])
        for copy in range(pieces.shape[0])
    ]
    for copy in copies:
        copy.start()
    offsets_copy.wait()
    rows = onehot.shape[0]
    pair = place // 2 * 2
    position = place * rows + lax.broadcasted_iota(jnp.int32, onehot.shape, 0)
    start = jnp.where(position >= offsets[pair + 1], offsets[pair + 1], offsets[pair])
    local = position - start
    window = local >> 2
    quarter = local & 3
    half = WIDTH // 2
    token_row = 2 * (window // half) + (quarter >> 1)
    token_col = 2 * (window % half) + (quarter & 1)
    lane = lax.broadcasted_iota(jnp.int32, onehot.shape, 1)
    chosen = lane == jnp.where(lane < side, token_row, token_col + side)
    onehot[...] = jnp.where(chosen, 1.0, 0.0).astype(jnp.bfloat16)
    for copy in copies + loads:
        copy.wait()


def front_kernel(
    onehot, patches, tables, weight, resid_hbm, queries, pairs, resid, resid_sems
):
    embedded = dot(onehot[...], tables[...], ((1,), (0,)))
    values = patches[...].astype(jnp.float32) + embedded
    resid_copies = []
    for tile in range(resid.shape[0]):
        resid[tile] = values[:, tile * LANES : (tile + 1) * LANES]
        resid_copies.append(
            pltpu.make_async_copy(resid.at[tile], resid_hbm.at[tile], resid_sems.at[tile])
        )
        resid_copies[-1].start()
    normed = normalize(values).astype(jnp.bfloat16)
    width = weight.shape[1]
    wide = weight[...].reshape(3 * width, weight.shape[2])
    out = dot(wide, normed, ((1,), (1,))).astype(jnp.bfloat16)
    queries[...] = out[:width]
    pairs[...] = out[width:]
    for copy in resid_copies:
        copy.wait()


def block_scores(offsets, block, query, other):
    rows = query.shape[1]
    place = lax.axis_index("tok")
    border = offsets[place // 2 * 2 + 1]
    key_place = jnp.where(place % 2 == 0, place + 1, place - 1) if other else place
    query_pos = place * rows + lax.broadcasted_iota(jnp.int32, (1, rows), 1)
    key_pos = key_place * rows + lax.broadcasted_iota(jnp.int32, (rows, 1), 0)
    query_side = jnp.where(query_pos >= border, 1, 0)
    key_side = jnp.where(key_pos >= border, 1, 0)
    scores = dot(block, query, ((0,), (0,))) * SCALE
    return jnp.where(key_side == query_side, scores, MASKED)


def near_kernel(offsets, queries, near, mixed, stats):
    width = queries.shape[0]
    for head in range(width // HEAD_DIM):
        own = slice(head * HEAD_DIM, (head + 1) * HEAD_DIM)
        value = slice(width + head * HEAD_DIM, width + (head + 1) * HEAD_DIM)
        scores = block_scores(offsets, near[own, :], queries[own, :], False)
        top = jnp.max(scores, axis=0, keepdims=True)
        expo = jnp.exp(scores - top)
        stats[2 * head : 2 * head + 1, :] = top
        stats[2 * head + 1 : 2 * head + 2, :] = jnp.sum(expo, axis=0, keepdims=True)
        mixed[own, :] = dot(near[value, :], expo.astype(jnp.bfloat16), ((1,), (0,)))


def far_kernel(offsets, queries, far, near_mixed, stats, out, attended, sems):
    width = queries.shape[0]
    copies = []
    for head in range(width // HEAD_DIM):
        own = slice(head * HEAD_DIM, (head + 1) * HEAD_DIM)
        value = slice(width + head * HEAD_DIM, width + (head + 1) * HEAD_DIM)
        scores = block_scores(offsets, far[own, :], queries[own, :], True)
        near_top = stats[2 * head : 2 * head + 1, :]
        top = jnp.maximum(near_top, jnp.max(scores, axis=0, keepdims=True))
        expo = jnp.exp(scores - top)
        scale = jnp.exp(near_top - top)
        total = stats[2 * head + 1 : 2 * head + 2, :] * scale
        total += jnp.sum(expo, axis=0, keepdims=True)
        mixed = near_mixed[own, :] * scale
        mixed += dot(far[value, :], expo.astype(jnp.bfloat16), ((1,), (0,)))
        attended[own, :] = (mixed / total).astype(jnp.bfloat16)
        part = pl.ds(head * HEAD_DIM, HEAD_DIM)
        for copy in range(out.shape[0]):
            copies.append(
                pltpu.make_async_copy(
                    attended.at[part, :], out.at[copy, part, :], sems.at[head, copy]
                )
            )
            copies[-1].start()
    for copy in copies:
        copy.wait()


def project_kernel(
    gathered,
    weight,
    resid_hbm,
    merge_hbm,
    attended,
    partial,
    merge_weight,
    resid,
    resid_sems,
    merge_sems,
):
    resid_copies = [
        pltpu.make_async_copy(resid_hbm.at[tile], resid.at[tile], resid_sems.at[tile])
        for tile in range(resid.shape[0])
    ]
    depth = merge_weight.shape[0] // 4
    merge_copies = [
        pltpu.make_async_copy(
            merge_hbm.at[pl.ds(i * depth, depth), :],
            merge_weight.at[pl.ds(i * depth, depth), :],
            merge_sems.at[i],
        )
        for i in range(4)
    ]
    for copy in resid_copies + merge_copies:
        copy.start()
    core = lax.axis_index("tok") % 2
    group, depth, rows = gathered.shape
    whole = gathered[...].reshape(group * depth, rows)
    tiles = resid.shape[0]
    for tile in range(tiles):
        part = slice(tile * LANES, (tile + 1) * LANES)
        attended[:, part] = whole[part, :].T
    part = dot(attended[...], weight[...], ((1,), (0,)))
    for copy in resid_copies:
        copy.wait()
    for tile in range(tiles // 2):
        place = core * (tiles // 2) + tile
        partial[place] = resid[place] + part[:, tile * LANES : (tile + 1) * LANES]
        place = (1 - core) * (tiles // 2) + tile
        partial[place] = resid[place]
    for copy in merge_copies:
        copy.wait()


def merge_kernel(
    attended, weight_hbm, partial, merge_weight, out, weight, total, block, weight_sems, sems
):
    chunks = [(start, min(256, weight.shape[1] - start)) for start in range(0, weight.shape[1], 256)]
    loads = [
        pltpu.make_async_copy(
            weight_hbm.at[:, pl.ds(start, size)],
            weight.at[:, pl.ds(start, size)],
            weight_sems.at[chunk],
        )
        for chunk, (start, size) in enumerate(chunks)
    ]
    for load in loads:
        load.start()
    core = lax.axis_index("tok") % 2
    tiles, rows = partial.shape[:2]
    for tile in range(tiles // 2):
        place = core * (tiles // 2) + tile
        total[place] = partial[place]
    for load, (start, size) in zip(loads, chunks):
        load.wait()
        part = dot(attended[...], weight[:, start : start + size], ((1,), (0,)))
        for tile in range(size // LANES):
            place = (1 - core) * (tiles // 2) + start // LANES + tile
            total[place] = partial[place] + part[:, tile * LANES : (tile + 1) * LANES]
    values = jnp.concatenate([total[tile] for tile in range(tiles)], axis=1)
    normed = normalize(values)
    for tile in range(tiles):
        total[tile] = normed[:, tile * LANES : (tile + 1) * LANES]
    width = tiles * LANES
    projected = jnp.zeros(block.shape, jnp.float32)
    for quarter in range(4):
        part = [total[tile, pl.ds(quarter, rows // 4, stride=4), :] for tile in range(tiles)]
        part = jnp.concatenate(part, axis=1).astype(jnp.bfloat16)
        weight = merge_weight[:, quarter * width : (quarter + 1) * width]
        projected += dot(weight, part, ((1,), (1,)))
    block[...] = projected.astype(block.dtype)
    copies = [
        pltpu.make_async_copy(block, out.at[copy], sems.at[copy]) for copy in range(out.shape[0])
    ]
    for copy in copies:
        copy.start()
    for copy in copies:
        copy.wait()


def pick_kernel(wanted, blocks, out, sems):
    copies = [
        pltpu.make_async_copy(blocks.at[wanted[slot]], out.at[slot], sems.at[slot])
        for slot in range(out.shape[0])
    ]
    for copy in copies:
        copy.start()
    for copy in copies:
        copy.wait()


def deliver_kernel(facts, blocks, out):
    source = 2 * facts[0]
    pair = jnp.concatenate([blocks[source], blocks[source + 1]], axis=1)
    shape = (pair.shape[1], out.shape[1])
    row = lax.broadcasted_iota(jnp.int32, shape, 0) - facts[1]
    slot = lax.broadcasted_iota(jnp.int32, shape, 1)
    chosen = row == jnp.where(slot < facts[2], slot, -shape[0])
    chosen = jnp.where(chosen, 1.0, 0.0).astype(jnp.bfloat16)
    out[...] = dot(pair, chosen, ((1,), (0,))).astype(out.dtype)


def on_device(
    patches,
    row_table,
    col_table,
    qkv_weight,
    out_weight,
    merge_weight,
    segment_ids,
    image_grids,
    image_offsets,
    owners,
):
    block_rows, width = patches.shape
    width_here = qkv_weight.shape[1]
    group = lax.axis_size("head")
    places = lax.axis_size("tok")
    place = lax.axis_index("tok")
    params = pltpu.CompilerParams(vmem_limit_bytes=24 * 2**20)
    at_hbm = lambda x: pltpu.with_memory_space_constraint(x, pltpu.HBM)

    sides = places // (RING * 2)
    tok_of = [[[(x * RING + y) * 2 + c for c in range(2)] for y in range(RING)] for x in range(sides)]
    rings_y = [[tok_of[x][y][c] for y in range(RING)] for x in range(sides) for c in range(2)]
    rings_x = [[tok_of[x][y][c] for x in range(sides)] for y in range(RING) for c in range(2)]
    planes = [[tok_of[x][y][c] for x in range(sides) for c in range(2)] for y in range(RING)]
    my_x = place // (2 * RING)
    my_y = place // 2 % RING
    core = place % 2

    depth, columns = width_here // sides, width // 2
    tables_shape = (2 * row_table.shape[0], width)
    pieces, tables, qkv_here, onehot = pl.pallas_call(
        load_kernel,
        out_shape=(
            pltpu.HBM((group, depth, columns), jnp.bfloat16),
            jax.ShapeDtypeStruct(tables_shape, jnp.bfloat16),
            jax.ShapeDtypeStruct(qkv_weight.shape, jnp.bfloat16),
            jax.ShapeDtypeStruct((block_rows, 2 * row_table.shape[0]), jnp.bfloat16),
        ),
        in_specs=[HBM] * 5,
        out_specs=(HBM, VMEM, VMEM, VMEM),
        scratch_shapes=[
            pltpu.VMEM((depth, columns), jnp.bfloat16),
            pltpu.SMEM(image_offsets.shape, jnp.int32),
            pltpu.SemaphoreType.DMA((3 + qkv_weight.shape[0],)),
            pltpu.SemaphoreType.DMA((group + 1,)),
        ],
        compiler_params=params,
    )(*map(at_hbm, (out_weight, row_table, col_table, qkv_weight, image_offsets)))
    pieces = lax.all_to_all(pieces, "head", 0, 0, tiled=True)

    resid, queries, near = pl.pallas_call(
        front_kernel,
        out_shape=(
            pltpu.HBM((width // LANES, block_rows, LANES), jnp.float32),
            jax.ShapeDtypeStruct((width_here, block_rows), jnp.bfloat16),
            jax.ShapeDtypeStruct((2 * width_here, block_rows), jnp.bfloat16),
        ),
        in_specs=[VMEM, VMEM, VMEM, VMEM],
        out_specs=(HBM, VMEM, VMEM),
        scratch_shapes=[
            pltpu.VMEM((width // LANES, block_rows, LANES), jnp.float32),
            pltpu.SemaphoreType.DMA((width // LANES,)),
        ],
        compiler_params=params,
        cost_estimate=pl.CostEstimate(
            flops=3 * 2 * block_rows * width * width_here, bytes_accessed=8 * 2**20, transcendentals=0
        ),
    )(onehot, patches, tables, qkv_here)
    far = partner(near, "tok", 0)
    mixed, stats = pl.pallas_call(
        near_kernel,
        out_shape=(
            jax.ShapeDtypeStruct((width_here, block_rows), jnp.float32),
            jax.ShapeDtypeStruct((2 * width_here // HEAD_DIM, block_rows), jnp.float32),
        ),
        in_specs=[SMEM, VMEM, VMEM],
        out_specs=(VMEM, VMEM),
        compiler_params=params,
        cost_estimate=pl.CostEstimate(
            flops=4 * block_rows * block_rows * width_here,
            bytes_accessed=2**21,
            transcendentals=block_rows * block_rows * 2,
        ),
    )(image_offsets, queries, near)
    sent = pl.pallas_call(
        far_kernel,
        out_shape=pltpu.HBM((group, width_here, block_rows), jnp.bfloat16),
        in_specs=[SMEM, VMEM, VMEM, VMEM, VMEM],
        out_specs=HBM,
        scratch_shapes=[
            pltpu.VMEM((width_here, block_rows), jnp.bfloat16),
            pltpu.SemaphoreType.DMA((width_here // HEAD_DIM, group)),
        ],
        compiler_params=params,
    )(image_offsets, queries, far, mixed, stats)
    pieces, sent = lax.optimization_barrier((pieces, sent))
    own_weight = [
        lax.all_gather(part, "tok", axis=1, axis_index_groups=rings_x, tiled=True)
        for part in jnp.split(pieces, 2)
    ]
    own_weight = jnp.concatenate(own_weight, axis=0).reshape(group * width_here, columns)
    other_weight = partner(own_weight, "tok", 0)

    gathered = lax.all_to_all(sent, "head", 0, 0, tiled=True)
    rows_here = block_rows // 4
    blocks_shape = pltpu.HBM((RING, width_here, rows_here), jnp.bfloat16)
    tiles = width // LANES
    half_flops = 2 * block_rows * width * columns
    attended, partial, merge_here = pl.pallas_call(
        project_kernel,
        out_shape=(
            jax.ShapeDtypeStruct((block_rows, width), jnp.bfloat16),
            jax.ShapeDtypeStruct((tiles, block_rows, LANES), jnp.float32),
            jax.ShapeDtypeStruct(merge_weight.shape, jnp.bfloat16),
        ),
        in_specs=[VMEM, VMEM, HBM, HBM],
        out_specs=(VMEM, VMEM, VMEM),
        scratch_shapes=[
            pltpu.VMEM((tiles, block_rows, LANES), jnp.float32),
            pltpu.SemaphoreType.DMA((tiles,)),
            pltpu.SemaphoreType.DMA((4,)),
        ],
        compiler_params=params,
        cost_estimate=pl.CostEstimate(
            flops=half_flops, bytes_accessed=8 * 2**20, transcendentals=0
        ),
    )(gathered, own_weight, at_hbm(resid), at_hbm(merge_weight))
    projected = pl.pallas_call(
        merge_kernel,
        out_shape=blocks_shape,
        in_specs=[VMEM, HBM, VMEM, VMEM],
        out_specs=HBM,
        scratch_shapes=[
            pltpu.VMEM(other_weight.shape, jnp.bfloat16),
            pltpu.VMEM((tiles, block_rows, LANES), jnp.float32),
            pltpu.VMEM((width_here, rows_here), jnp.bfloat16),
            pltpu.SemaphoreType.DMA((columns // 256 + 1,)),
            pltpu.SemaphoreType.DMA((RING,)),
        ],
        compiler_params=params,
    )(attended, at_hbm(other_weight), partial, merge_here)

    image_ids = jnp.arange(owners.shape[0], dtype=jnp.int32)
    place_ids = jnp.arange(places, dtype=jnp.int32)
    image_of = jnp.sum(jnp.where(owners[None, :] == place_ids[:, None], image_ids[None, :], 0), axis=1)
    pair_y = (image_of // 2 % RING).reshape(sides, RING, 2)
    wanted = jnp.sum(
        jnp.where((jnp.arange(RING) == my_y)[None, :, None], pair_y, 0), axis=1
    ).reshape(2 * sides)
    mine = owners == place
    tokens = image_grids[:, 0] * image_grids[:, 1]
    first_token = image_offsets - image_ids // 2 * (2 * block_rows)
    facts = jnp.stack([image_ids // 2 // RING, first_token // 4, tokens // 4])
    facts = jnp.sum(jnp.where(mine[None, :], facts, 0), axis=1)

    blocks = lax.all_to_all(projected, "tok", 0, 0, axis_index_groups=rings_y, tiled=True)
    blocks = pl.pallas_call(
        pick_kernel,
        out_shape=pltpu.HBM((2 * sides, width_here, rows_here), jnp.bfloat16),
        in_specs=[SMEM, ANY],
        out_specs=HBM,
        scratch_shapes=[pltpu.SemaphoreType.DMA((2 * sides,))],
        compiler_params=params,
    )(wanted, blocks)
    blocks = lax.all_to_all(blocks, "tok", 0, 0, axis_index_groups=planes, tiled=True)
    return pl.pallas_call(
        deliver_kernel,
        out_shape=jax.ShapeDtypeStruct((width_here, CAP), jnp.bfloat16),
        in_specs=[SMEM, VMEM],
        out_specs=VMEM,
        compiler_params=params,
    )(facts, blocks).T


def solution(mesh):
    placed = (
        P("tok", None),
        P(),
        P(),
        P(None, "head", None),
        P("head", None),
        P("head", None),
        P("tok"),
        P(),
        P(),
        P(),
    )
    return jax.shard_map(
        on_device, mesh=mesh, in_specs=placed, out_specs=P("tok", "head"), check_vma=False
    )
```

```python
import math

import jax
import jax.numpy as jnp
from jax import lax
from jax.experimental import pallas as pl
from jax.experimental.pallas import tpu as pltpu
from jax.sharding import PartitionSpec as P

HEAD_DIM = 80
CAP = 248
WIDTH = 16
LANES = 128
RING = 8
SCALE = 1.0 / math.sqrt(HEAD_DIM)
MASKED = -1e30

VMEM = pl.BlockSpec(memory_space=pltpu.VMEM)
SMEM = pl.BlockSpec(memory_space=pltpu.SMEM)
HBM = pl.BlockSpec(memory_space=pltpu.HBM)
ANY = pl.BlockSpec(memory_space=pl.ANY)


def partner(x, axis, apart):
    return lax.ppermute(x, axis, [(i, i ^ 1 << apart) for i in range(lax.axis_size(axis))])


def normalize(values):
    centered = values - jnp.mean(values, axis=-1, keepdims=True)
    variance = jnp.mean(centered * centered, axis=-1, keepdims=True)
    return centered * lax.rsqrt(variance + 1e-06)


def dot(left, right, dims):
    return lax.dot_general(left, right, (dims, ((), ())), preferred_element_type=jnp.float32)


def load_kernel(
    out_weight,
    row_hbm,
    col_hbm,
    qkv_hbm,
    offsets_hbm,
    pieces,
    tables,
    qkv_weight,
    onehot,
    piece,
    offsets,
    sems,
    piece_sems,
):
    depth, columns = piece.shape
    side = row_hbm.shape[0]
    place = lax.axis_index("tok")
    row = pl.multiple_of(place // (2 * RING) * depth, 8)
    column = pl.multiple_of(place % 2 * columns, LANES)
    first = pltpu.make_async_copy(
        out_weight.at[pl.ds(row, depth), pl.ds(column, columns)], piece, sems.at[0]
    )
    first.start()
    offsets_copy = pltpu.make_async_copy(offsets_hbm, offsets, piece_sems.at[pieces.shape[0]])
    offsets_copy.start()
    loads = [
        pltpu.make_async_copy(row_hbm, tables.at[pl.ds(0, side), :], sems.at[1]),
        pltpu.make_async_copy(col_hbm, tables.at[pl.ds(side, side), :], sems.at[2]),
    ]
    for part in range(qkv_hbm.shape[0]):
        loads.append(
            pltpu.make_async_copy(qkv_hbm.at[part], qkv_weight.at[part], sems.at[3 + part])
        )
    for load in loads:
        load.start()
    first.wait()
    copies = [
        pltpu.make_async_copy(piece, pieces.at[copy], piece_sems.at[copy])
        for copy in range(pieces.shape[0])
    ]
    for copy in copies:
        copy.start()
    offsets_copy.wait()
    rows = onehot.shape[0]
    pair = place // 2 * 2
    position = place * rows + lax.broadcasted_iota(jnp.int32, onehot.shape, 0)
    start = jnp.where(position >= offsets[pair + 1], offsets[pair + 1], offsets[pair])
    local = position - start
    window = local >> 2
    quarter = local & 3
    half = WIDTH // 2
    token_row = 2 * (window // half) + (quarter >> 1)
    token_col = 2 * (window % half) + (quarter & 1)
    lane = lax.broadcasted_iota(jnp.int32, onehot.shape, 1)
    chosen = lane == jnp.where(lane < side, token_row, token_col + side)
    onehot[...] = jnp.where(chosen, 1.0, 0.0).astype(jnp.bfloat16)
    for copy in copies + loads:
        copy.wait()


def front_kernel(
    onehot, patches, tables, weight, resid_hbm, queries, pairs, resid, resid_sems
):
    embedded = dot(onehot[...], tables[...], ((1,), (0,)))
    values = patches[...].astype(jnp.float32) + embedded
    resid_copies = []
    for tile in range(resid.shape[0]):
        resid[tile] = values[:, tile * LANES : (tile + 1) * LANES]
        resid_copies.append(
            pltpu.make_async_copy(resid.at[tile], resid_hbm.at[tile], resid_sems.at[tile])
        )
        resid_copies[-1].start()
    normed = normalize(values).astype(jnp.bfloat16)
    width = weight.shape[1]
    wide = weight[...].reshape(3 * width, weight.shape[2])
    out = dot(wide, normed, ((1,), (1,))).astype(jnp.bfloat16)
    queries[...] = out[:width]
    pairs[...] = out[width:]
    for copy in resid_copies:
        copy.wait()


def block_scores(offsets, block, query, other):
    rows = query.shape[1]
    place = lax.axis_index("tok")
    border = offsets[place // 2 * 2 + 1]
    key_place = jnp.where(place % 2 == 0, place + 1, place - 1) if other else place
    query_pos = place * rows + lax.broadcasted_iota(jnp.int32, (1, rows), 1)
    key_pos = key_place * rows + lax.broadcasted_iota(jnp.int32, (rows, 1), 0)
    query_side = jnp.where(query_pos >= border, 1, 0)
    key_side = jnp.where(key_pos >= border, 1, 0)
    scores = dot(block, query, ((0,), (0,))) * SCALE
    return jnp.where(key_side == query_side, scores, MASKED)


def near_kernel(offsets, queries, near, mixed, stats):
    width = queries.shape[0]
    for head in range(width // HEAD_DIM):
        own = slice(head * HEAD_DIM, (head + 1) * HEAD_DIM)
        value = slice(width + head * HEAD_DIM, width + (head + 1) * HEAD_DIM)
        scores = block_scores(offsets, near[own, :], queries[own, :], False)
        top = jnp.max(scores, axis=0, keepdims=True)
        expo = jnp.exp(scores - top)
        stats[2 * head : 2 * head + 1, :] = top
        stats[2 * head + 1 : 2 * head + 2, :] = jnp.sum(expo, axis=0, keepdims=True)
        mixed[own, :] = dot(near[value, :], expo.astype(jnp.bfloat16), ((1,), (0,)))


def far_kernel(offsets, queries, far, near_mixed, stats, out, attended, sems):
    width = queries.shape[0]
    copies = []
    for head in range(width // HEAD_DIM):
        own = slice(head * HEAD_DIM, (head + 1) * HEAD_DIM)
        value = slice(width + head * HEAD_DIM, width + (head + 1) * HEAD_DIM)
        scores = block_scores(offsets, far[own, :], queries[own, :], True)
        near_top = stats[2 * head : 2 * head + 1, :]
        top = jnp.maximum(near_top, jnp.max(scores, axis=0, keepdims=True))
        expo = jnp.exp(scores - top)
        scale = jnp.exp(near_top - top)
        total = stats[2 * head + 1 : 2 * head + 2, :] * scale
        total += jnp.sum(expo, axis=0, keepdims=True)
        mixed = near_mixed[own, :] * scale
        mixed += dot(far[value, :], expo.astype(jnp.bfloat16), ((1,), (0,)))
        attended[own, :] = (mixed / total).astype(jnp.bfloat16)
        part = pl.ds(head * HEAD_DIM, HEAD_DIM)
        for copy in range(out.shape[0]):
            copies.append(
                pltpu.make_async_copy(
                    attended.at[part, :], out.at[copy, part, :], sems.at[head, copy]
                )
            )
            copies[-1].start()
    for copy in copies:
        copy.wait()


def turn_kernel(
    gathered, resid_hbm, merge_hbm, attended, resid, merge_weight, resid_sems, merge_sems
):
    tiles = resid.shape[0]
    loads = [
        pltpu.make_async_copy(resid_hbm.at[tile], resid.at[tile], resid_sems.at[tile])
        for tile in range(tiles)
    ]
    depth = merge_weight.shape[0] // 4
    for i in range(4):
        part = pl.ds(i * depth, depth)
        loads.append(
            pltpu.make_async_copy(merge_hbm.at[part, :], merge_weight.at[part, :], merge_sems.at[i])
        )
    for load in loads:
        load.start()
    whole = gathered[...].reshape(gathered.shape[0] * gathered.shape[1], gathered.shape[2])
    for tile in range(tiles):
        part = slice(tile * LANES, (tile + 1) * LANES)
        attended[:, part] = whole[part, :].T
    for load in loads:
        load.wait()


def merge_kernel(
    attended,
    own_weight,
    other_hbm,
    resid,
    merge_weight,
    out,
    other_weight,
    total,
    block,
    other_sems,
    sems,
):
    columns = own_weight.shape[1]
    chunks = [(start, min(256, columns - start)) for start in range(0, columns, 256)]
    loads = [
        pltpu.make_async_copy(
            other_hbm.at[:, pl.ds(start, size)],
            other_weight.at[:, pl.ds(start, size)],
            other_sems.at[chunk],
        )
        for chunk, (start, size) in enumerate(chunks)
    ]
    for load in loads:
        load.start()
    core = lax.axis_index("tok") % 2
    tiles, rows = resid.shape[:2]
    part = dot(attended[...], own_weight[...], ((1,), (0,)))
    for tile in range(tiles // 2):
        place = core * (tiles // 2) + tile
        total[place] = resid[place] + part[:, tile * LANES : (tile + 1) * LANES]
    for load, (start, size) in zip(loads, chunks):
        load.wait()
        part = dot(attended[...], other_weight[:, start : start + size], ((1,), (0,)))
        for tile in range(size // LANES):
            place = (1 - core) * (tiles // 2) + start // LANES + tile
            total[place] = resid[place] + part[:, tile * LANES : (tile + 1) * LANES]
    values = jnp.concatenate([total[tile] for tile in range(tiles)], axis=1)
    normed = normalize(values)
    for tile in range(tiles):
        total[tile] = normed[:, tile * LANES : (tile + 1) * LANES]
    width = tiles * LANES
    projected = jnp.zeros(block.shape, jnp.float32)
    for quarter in range(4):
        part = [total[tile, pl.ds(quarter, rows // 4, stride=4), :] for tile in range(tiles)]
        part = jnp.concatenate(part, axis=1).astype(jnp.bfloat16)
        weight = merge_weight[:, quarter * width : (quarter + 1) * width]
        projected += dot(weight, part, ((1,), (1,)))
    block[...] = projected.astype(block.dtype)
    copies = [
        pltpu.make_async_copy(block, out.at[copy], sems.at[copy]) for copy in range(out.shape[0])
    ]
    for copy in copies:
        copy.start()
    for copy in copies:
        copy.wait()


def pick_kernel(wanted, blocks, out, sems):
    copies = [
        pltpu.make_async_copy(blocks.at[wanted[slot]], out.at[slot], sems.at[slot])
        for slot in range(out.shape[0])
    ]
    for copy in copies:
        copy.start()
    for copy in copies:
        copy.wait()


def deliver_kernel(facts, blocks, out):
    source = 2 * facts[0]
    pair = jnp.concatenate([blocks[source], blocks[source + 1]], axis=1)
    shape = (pair.shape[1], out.shape[1])
    row = lax.broadcasted_iota(jnp.int32, shape, 0) - facts[1]
    slot = lax.broadcasted_iota(jnp.int32, shape, 1)
    chosen = row == jnp.where(slot < facts[2], slot, -shape[0])
    chosen = jnp.where(chosen, 1.0, 0.0).astype(jnp.bfloat16)
    out[...] = dot(pair, chosen, ((1,), (0,))).astype(out.dtype)


def on_device(
    patches,
    row_table,
    col_table,
    qkv_weight,
    out_weight,
    merge_weight,
    segment_ids,
    image_grids,
    image_offsets,
    owners,
):
    block_rows, width = patches.shape
    width_here = qkv_weight.shape[1]
    group = lax.axis_size("head")
    places = lax.axis_size("tok")
    place = lax.axis_index("tok")
    params = pltpu.CompilerParams(vmem_limit_bytes=24 * 2**20)
    at_hbm = lambda x: pltpu.with_memory_space_constraint(x, pltpu.HBM)

    sides = places // (RING * 2)
    tok_of = [[[(x * RING + y) * 2 + c for c in range(2)] for y in range(RING)] for x in range(sides)]
    rings_y = [[tok_of[x][y][c] for y in range(RING)] for x in range(sides) for c in range(2)]
    rings_x = [[tok_of[x][y][c] for x in range(sides)] for y in range(RING) for c in range(2)]
    planes = [[tok_of[x][y][c] for x in range(sides) for c in range(2)] for y in range(RING)]
    my_x = place // (2 * RING)
    my_y = place // 2 % RING
    core = place % 2

    depth, columns = width_here // sides, width // 2
    tables_shape = (2 * row_table.shape[0], width)
    pieces, tables, qkv_here, onehot = pl.pallas_call(
        load_kernel,
        out_shape=(
            pltpu.HBM((group, depth, columns), jnp.bfloat16),
            jax.ShapeDtypeStruct(tables_shape, jnp.bfloat16),
            jax.ShapeDtypeStruct(qkv_weight.shape, jnp.bfloat16),
            jax.ShapeDtypeStruct((block_rows, 2 * row_table.shape[0]), jnp.bfloat16),
        ),
        in_specs=[HBM] * 5,
        out_specs=(HBM, VMEM, VMEM, VMEM),
        scratch_shapes=[
            pltpu.VMEM((depth, columns), jnp.bfloat16),
            pltpu.SMEM(image_offsets.shape, jnp.int32),
            pltpu.SemaphoreType.DMA((3 + qkv_weight.shape[0],)),
            pltpu.SemaphoreType.DMA((group + 1,)),
        ],
        compiler_params=params,
    )(*map(at_hbm, (out_weight, row_table, col_table, qkv_weight, image_offsets)))
    pieces = lax.all_to_all(pieces, "head", 0, 0, tiled=True)

    resid, queries, near = pl.pallas_call(
        front_kernel,
        out_shape=(
            pltpu.HBM((width // LANES, block_rows, LANES), jnp.float32),
            jax.ShapeDtypeStruct((width_here, block_rows), jnp.bfloat16),
            jax.ShapeDtypeStruct((2 * width_here, block_rows), jnp.bfloat16),
        ),
        in_specs=[VMEM, VMEM, VMEM, VMEM],
        out_specs=(HBM, VMEM, VMEM),
        scratch_shapes=[
            pltpu.VMEM((width // LANES, block_rows, LANES), jnp.float32),
            pltpu.SemaphoreType.DMA((width // LANES,)),
        ],
        compiler_params=params,
        cost_estimate=pl.CostEstimate(
            flops=3 * 2 * block_rows * width * width_here, bytes_accessed=8 * 2**20, transcendentals=0
        ),
    )(onehot, patches, tables, qkv_here)
    far = partner(near, "tok", 0)
    mixed, stats = pl.pallas_call(
        near_kernel,
        out_shape=(
            jax.ShapeDtypeStruct((width_here, block_rows), jnp.float32),
            jax.ShapeDtypeStruct((2 * width_here // HEAD_DIM, block_rows), jnp.float32),
        ),
        in_specs=[SMEM, VMEM, VMEM],
        out_specs=(VMEM, VMEM),
        compiler_params=params,
        cost_estimate=pl.CostEstimate(
            flops=4 * block_rows * block_rows * width_here,
            bytes_accessed=2**21,
            transcendentals=block_rows * block_rows * 2,
        ),
    )(image_offsets, queries, near)
    sent = pl.pallas_call(
        far_kernel,
        out_shape=pltpu.HBM((group, width_here, block_rows), jnp.bfloat16),
        in_specs=[SMEM, VMEM, VMEM, VMEM, VMEM],
        out_specs=HBM,
        scratch_shapes=[
            pltpu.VMEM((width_here, block_rows), jnp.bfloat16),
            pltpu.SemaphoreType.DMA((width_here // HEAD_DIM, group)),
        ],
        compiler_params=params,
    )(image_offsets, queries, far, mixed, stats)
    pieces, _ = lax.optimization_barrier((pieces, sent))
    own_weight = [
        lax.all_gather(part, "tok", axis=1, axis_index_groups=rings_x, tiled=True)
        for part in jnp.split(pieces, 2)
    ]
    own_weight = jnp.concatenate(own_weight, axis=0).reshape(group * width_here, columns)
    other_weight = partner(own_weight, "tok", 0)

    gathered = lax.all_to_all(sent, "head", 0, 0, tiled=True)
    rows_here = block_rows // 4
    blocks_shape = pltpu.HBM((RING, width_here, rows_here), jnp.bfloat16)
    tiles = width // LANES
    attended, resid, merge_here = pl.pallas_call(
        turn_kernel,
        out_shape=(
            jax.ShapeDtypeStruct((block_rows, width), jnp.bfloat16),
            jax.ShapeDtypeStruct((tiles, block_rows, LANES), jnp.float32),
            jax.ShapeDtypeStruct(merge_weight.shape, jnp.bfloat16),
        ),
        in_specs=[VMEM, HBM, HBM],
        out_specs=(VMEM, VMEM, VMEM),
        scratch_shapes=[
            pltpu.SemaphoreType.DMA((tiles,)),
            pltpu.SemaphoreType.DMA((4,)),
        ],
        compiler_params=params,
        cost_estimate=pl.CostEstimate(
            flops=2 * block_rows * width * columns, bytes_accessed=8 * 2**20, transcendentals=0
        ),
    )(gathered, at_hbm(resid), at_hbm(merge_weight))
    projected = pl.pallas_call(
        merge_kernel,
        out_shape=blocks_shape,
        in_specs=[VMEM, VMEM, HBM, VMEM, VMEM],
        out_specs=HBM,
        scratch_shapes=[
            pltpu.VMEM(other_weight.shape, jnp.bfloat16),
            pltpu.VMEM((tiles, block_rows, LANES), jnp.float32),
            pltpu.VMEM((width_here, rows_here), jnp.bfloat16),
            pltpu.SemaphoreType.DMA((columns // 256 + 1,)),
            pltpu.SemaphoreType.DMA((RING,)),
        ],
        compiler_params=params,
    )(attended, own_weight, at_hbm(other_weight), resid, merge_here)

    image_ids = jnp.arange(owners.shape[0], dtype=jnp.int32)
    place_ids = jnp.arange(places, dtype=jnp.int32)
    image_of = jnp.sum(jnp.where(owners[None, :] == place_ids[:, None], image_ids[None, :], 0), axis=1)
    pair_y = (image_of // 2 % RING).reshape(sides, RING, 2)
    wanted = jnp.sum(
        jnp.where((jnp.arange(RING) == my_y)[None, :, None], pair_y, 0), axis=1
    ).reshape(2 * sides)
    mine = owners == place
    tokens = image_grids[:, 0] * image_grids[:, 1]
    first_token = image_offsets - image_ids // 2 * (2 * block_rows)
    facts = jnp.stack([image_ids // 2 // RING, first_token // 4, tokens // 4])
    facts = jnp.sum(jnp.where(mine[None, :], facts, 0), axis=1)

    blocks = lax.all_to_all(projected, "tok", 0, 0, axis_index_groups=rings_y, tiled=True)
    blocks = pl.pallas_call(
        pick_kernel,
        out_shape=pltpu.HBM((2 * sides, width_here, rows_here), jnp.bfloat16),
        in_specs=[SMEM, ANY],
        out_specs=HBM,
        scratch_shapes=[pltpu.SemaphoreType.DMA((2 * sides,))],
        compiler_params=params,
    )(wanted, blocks)
    blocks = lax.all_to_all(blocks, "tok", 0, 0, axis_index_groups=planes, tiled=True)
    return pl.pallas_call(
        deliver_kernel,
        out_shape=jax.ShapeDtypeStruct((width_here, CAP), jnp.bfloat16),
        in_specs=[SMEM, VMEM],
        out_specs=VMEM,
        compiler_params=params,
    )(facts, blocks).T


def solution(mesh):
    placed = (
        P("tok", None),
        P(),
        P(),
        P(None, "head", None),
        P("head", None),
        P("head", None),
        P("tok"),
        P(),
        P(),
        P(),
    )
    return jax.shard_map(
        on_device, mesh=mesh, in_specs=placed, out_specs=P("tok", "head"), check_vma=False
    )
```

```python
import math

import jax
import jax.numpy as jnp
from jax import lax
from jax.experimental import pallas as pl
from jax.experimental.pallas import tpu as pltpu
from jax.sharding import PartitionSpec as P

HEAD_DIM = 80
CAP = 248
WIDTH = 16
LANES = 128
RING = 8
SCALE = 1.0 / math.sqrt(HEAD_DIM)
MASKED = -1e30

VMEM = pl.BlockSpec(memory_space=pltpu.VMEM)
SMEM = pl.BlockSpec(memory_space=pltpu.SMEM)
HBM = pl.BlockSpec(memory_space=pltpu.HBM)
ANY = pl.BlockSpec(memory_space=pl.ANY)


def partner(x, axis, apart):
    return lax.ppermute(x, axis, [(i, i ^ 1 << apart) for i in range(lax.axis_size(axis))])


def normalize(values):
    centered = values - jnp.mean(values, axis=-1, keepdims=True)
    variance = jnp.mean(centered * centered, axis=-1, keepdims=True)
    return centered * lax.rsqrt(variance + 1e-06)


def dot(left, right, dims):
    return lax.dot_general(left, right, (dims, ((), ())), preferred_element_type=jnp.float32)


def front_kernel(
    offsets_hbm,
    patches,
    row_hbm,
    col_hbm,
    weight_hbm,
    resid_hbm,
    queries,
    pairs,
    resid,
    tables,
    weight,
    offsets,
    sems,
):
    rows = patches.shape[0]
    side = tables.shape[0] // 2
    copies = [
        pltpu.make_async_copy(row_hbm, tables.at[pl.ds(0, side), :], sems.at[0]),
        pltpu.make_async_copy(col_hbm, tables.at[pl.ds(side, side), :], sems.at[1]),
        pltpu.make_async_copy(weight_hbm, weight, sems.at[2]),
    ]
    offsets_copy = pltpu.make_async_copy(offsets_hbm, offsets, sems.at[4])
    offsets_copy.start()
    for copy in copies:
        copy.start()
    offsets_copy.wait()
    place = lax.axis_index("tok")
    first = place // 2 * 2
    position = place * rows + lax.broadcasted_iota(jnp.int32, (rows, 2 * side), 0)
    start = jnp.where(position >= offsets[first + 1], offsets[first + 1], offsets[first])
    local = position - start
    window = local >> 2
    quarter = local & 3
    half = WIDTH // 2
    row = 2 * (window // half) + (quarter >> 1)
    col = 2 * (window % half) + (quarter & 1)
    lane = lax.broadcasted_iota(jnp.int32, (rows, 2 * side), 1)
    onehot = lane == jnp.where(lane < side, row, col + side)
    onehot = jnp.where(onehot, 1.0, 0.0).astype(jnp.bfloat16)
    copies[0].wait()
    copies[1].wait()
    embedded = dot(onehot, tables[...], ((1,), (0,)))
    values = patches[...].astype(jnp.float32) + embedded
    for tile in range(resid.shape[0]):
        resid[tile] = values[:, tile * LANES : (tile + 1) * LANES]
    resid_copy = pltpu.make_async_copy(resid, resid_hbm, sems.at[3])
    resid_copy.start()
    normed = normalize(values).astype(jnp.bfloat16)
    copies[2].wait()
    width = weight.shape[1]
    wide = weight[...].reshape(3 * width, weight.shape[2])
    out = dot(wide, normed, ((1,), (1,))).astype(jnp.bfloat16)
    queries[...] = out[:width]
    pairs[...] = out[width:]
    resid_copy.wait()


def block_scores(offsets, block, query, other):
    rows = query.shape[1]
    place = lax.axis_index("tok")
    border = offsets[place // 2 * 2 + 1]
    key_place = jnp.where(place % 2 == 0, place + 1, place - 1) if other else place
    query_pos = place * rows + lax.broadcasted_iota(jnp.int32, (1, rows), 1)
    key_pos = key_place * rows + lax.broadcasted_iota(jnp.int32, (rows, 1), 0)
    query_side = jnp.where(query_pos >= border, 1, 0)
    key_side = jnp.where(key_pos >= border, 1, 0)
    scores = dot(block, query, ((0,), (0,))) * SCALE
    return jnp.where(key_side == query_side, scores, MASKED)


def near_kernel(offsets, queries, near, mixed, stats):
    width = queries.shape[0]
    for head in range(width // HEAD_DIM):
        own = slice(head * HEAD_DIM, (head + 1) * HEAD_DIM)
        value = slice(width + head * HEAD_DIM, width + (head + 1) * HEAD_DIM)
        scores = block_scores(offsets, near[own, :], queries[own, :], False)
        top = jnp.max(scores, axis=0, keepdims=True)
        expo = jnp.exp(scores - top)
        stats[2 * head : 2 * head + 1, :] = top
        stats[2 * head + 1 : 2 * head + 2, :] = jnp.sum(expo, axis=0, keepdims=True)
        mixed[own, :] = dot(near[value, :], expo.astype(jnp.bfloat16), ((1,), (0,)))


def far_kernel(offsets, queries, far, near_mixed, stats, out, attended, sems):
    width = queries.shape[0]
    copies = []
    for head in range(width // HEAD_DIM):
        own = slice(head * HEAD_DIM, (head + 1) * HEAD_DIM)
        value = slice(width + head * HEAD_DIM, width + (head + 1) * HEAD_DIM)
        scores = block_scores(offsets, far[own, :], queries[own, :], True)
        near_top = stats[2 * head : 2 * head + 1, :]
        top = jnp.maximum(near_top, jnp.max(scores, axis=0, keepdims=True))
        expo = jnp.exp(scores - top)
        scale = jnp.exp(near_top - top)
        total = stats[2 * head + 1 : 2 * head + 2, :] * scale
        total += jnp.sum(expo, axis=0, keepdims=True)
        mixed = near_mixed[own, :] * scale
        mixed += dot(far[value, :], expo.astype(jnp.bfloat16), ((1,), (0,)))
        attended[own, :] = (mixed / total).astype(jnp.bfloat16)
        part = pl.ds(head * HEAD_DIM, HEAD_DIM)
        for copy in range(out.shape[0]):
            copies.append(
                pltpu.make_async_copy(
                    attended.at[part, :], out.at[copy, part, :], sems.at[head, copy]
                )
            )
            copies[-1].start()
    for copy in copies:
        copy.wait()


def project_kernel(
    gathered,
    weight,
    resid_hbm,
    merge_hbm,
    early_hbm,
    attended,
    partial,
    merge_weight,
    early,
    resid,
    sems,
):
    resid_copy = pltpu.make_async_copy(resid_hbm, resid, sems.at[0])
    resid_copy.start()
    merge_copy = pltpu.make_async_copy(merge_hbm, merge_weight, sems.at[1])
    merge_copy.start()
    early_copy = pltpu.make_async_copy(early_hbm, early, sems.at[2])
    early_copy.start()
    core = lax.axis_index("tok") % 2
    group, depth, rows = gathered.shape
    whole = gathered[...].reshape(group * depth, rows)
    tiles = resid.shape[0]
    for tile in range(tiles):
        part = slice(tile * LANES, (tile + 1) * LANES)
        attended[:, part] = whole[part, :].T
    part = dot(attended[...], weight[...], ((1,), (0,)))
    resid_copy.wait()
    for tile in range(tiles // 2):
        place = core * (tiles // 2) + tile
        partial[place] = resid[place] + part[:, tile * LANES : (tile + 1) * LANES]
        place = (1 - core) * (tiles // 2) + tile
        partial[place] = resid[place]
    merge_copy.wait()
    early_copy.wait()


def merge_kernel(
    attended, first_weight, second_weight, partial, merge_weight, out, total, block, sems
):
    core = lax.axis_index("tok") % 2
    tiles, rows = partial.shape[:2]
    depth = first_weight.shape[0]
    part = dot(attended[:, :depth], first_weight[...], ((1,), (0,)))
    part += dot(attended[:, depth:], second_weight[...], ((1,), (0,)))
    for tile in range(tiles // 2):
        place = core * (tiles // 2) + tile
        total[place] = partial[place]
        place = (1 - core) * (tiles // 2) + tile
        total[place] = partial[place] + part[:, tile * LANES : (tile + 1) * LANES]
    values = jnp.concatenate([total[tile] for tile in range(tiles)], axis=1)
    normed = normalize(values)
    for tile in range(tiles):
        total[tile] = normed[:, tile * LANES : (tile + 1) * LANES]
    width = tiles * LANES
    projected = jnp.zeros(block.shape, jnp.float32)
    for quarter in range(4):
        part = [total[tile, pl.ds(quarter, rows // 4, stride=4), :] for tile in range(tiles)]
        part = jnp.concatenate(part, axis=1).astype(jnp.bfloat16)
        weight = merge_weight[:, quarter * width : (quarter + 1) * width]
        projected += dot(weight, part, ((1,), (1,)))
    block[...] = projected.astype(block.dtype)
    copies = [
        pltpu.make_async_copy(block, out.at[copy], sems.at[copy]) for copy in range(out.shape[0])
    ]
    for copy in copies:
        copy.start()
    for copy in copies:
        copy.wait()


def pick_kernel(wanted, blocks, out, sems):
    copies = [
        pltpu.make_async_copy(blocks.at[wanted[slot]], out.at[slot], sems.at[slot])
        for slot in range(out.shape[0])
    ]
    for copy in copies:
        copy.start()
    for copy in copies:
        copy.wait()


def deliver_kernel(facts, blocks, out):
    source = 2 * facts[0]
    pair = jnp.concatenate([blocks[source], blocks[source + 1]], axis=1)
    shape = (pair.shape[1], out.shape[1])
    row = lax.broadcasted_iota(jnp.int32, shape, 0) - facts[1]
    slot = lax.broadcasted_iota(jnp.int32, shape, 1)
    chosen = row == jnp.where(slot < facts[2], slot, -shape[0])
    chosen = jnp.where(chosen, 1.0, 0.0).astype(jnp.bfloat16)
    out[...] = dot(pair, chosen, ((1,), (0,))).astype(out.dtype)


def on_device(
    patches,
    row_table,
    col_table,
    qkv_weight,
    out_weight,
    merge_weight,
    segment_ids,
    image_grids,
    image_offsets,
    owners,
):
    block_rows, width = patches.shape
    width_here = qkv_weight.shape[1]
    group = lax.axis_size("head")
    places = lax.axis_size("tok")
    place = lax.axis_index("tok")
    params = pltpu.CompilerParams(vmem_limit_bytes=24 * 2**20)
    at_hbm = lambda x: pltpu.with_memory_space_constraint(x, pltpu.HBM)

    sides = places // (RING * 2)
    tok_of = [[[(x * RING + y) * 2 + c for c in range(2)] for y in range(RING)] for x in range(sides)]
    rings_y = [[tok_of[x][y][c] for y in range(RING)] for x in range(sides) for c in range(2)]
    rings_x = [[tok_of[x][y][c] for x in range(sides)] for y in range(RING) for c in range(2)]
    planes = [[tok_of[x][y][c] for x in range(sides) for c in range(2)] for y in range(RING)]
    my_x = place // (2 * RING)
    my_y = place // 2 % RING
    core = place % 2

    depth, columns = width_here // sides, width // 2
    piece = lax.dynamic_slice(out_weight, (my_x * depth, core * columns), (depth, columns))
    pieces = jnp.broadcast_to(piece[None], (group, depth, columns))
    pieces = lax.all_to_all(pieces, "head", 0, 0, tiled=True)

    resid, queries, near = pl.pallas_call(
        front_kernel,
        out_shape=(
            pltpu.HBM((width // LANES, block_rows, LANES), jnp.float32),
            jax.ShapeDtypeStruct((width_here, block_rows), jnp.bfloat16),
            jax.ShapeDtypeStruct((2 * width_here, block_rows), jnp.bfloat16),
        ),
        in_specs=[HBM, VMEM, HBM, HBM, HBM],
        out_specs=(HBM, VMEM, VMEM),
        scratch_shapes=[
            pltpu.VMEM((width // LANES, block_rows, LANES), jnp.float32),
            pltpu.VMEM((2 * row_table.shape[0], width), jnp.bfloat16),
            pltpu.VMEM(qkv_weight.shape, jnp.bfloat16),
            pltpu.SMEM(image_offsets.shape, jnp.int32),
            pltpu.SemaphoreType.DMA((5,)),
        ],
        compiler_params=params,
        cost_estimate=pl.CostEstimate(
            flops=3 * 2 * block_rows * width * width_here, bytes_accessed=8 * 2**20, transcendentals=0
        ),
    )(at_hbm(image_offsets), patches, *map(at_hbm, (row_table, col_table, qkv_weight)))
    far = partner(near, "tok", 0)
    mixed, stats = pl.pallas_call(
        near_kernel,
        out_shape=(
            jax.ShapeDtypeStruct((width_here, block_rows), jnp.float32),
            jax.ShapeDtypeStruct((2 * width_here // HEAD_DIM, block_rows), jnp.float32),
        ),
        in_specs=[SMEM, VMEM, VMEM],
        out_specs=(VMEM, VMEM),
        compiler_params=params,
        cost_estimate=pl.CostEstimate(
            flops=4 * block_rows * block_rows * width_here,
            bytes_accessed=2**21,
            transcendentals=block_rows * block_rows * 2,
        ),
    )(image_offsets, queries, near)
    sent = pl.pallas_call(
        far_kernel,
        out_shape=pltpu.HBM((group, width_here, block_rows), jnp.bfloat16),
        in_specs=[SMEM, VMEM, VMEM, VMEM, VMEM],
        out_specs=HBM,
        scratch_shapes=[
            pltpu.VMEM((width_here, block_rows), jnp.bfloat16),
            pltpu.SemaphoreType.DMA((width_here // HEAD_DIM, group)),
        ],
        compiler_params=params,
    )(image_offsets, queries, far, mixed, stats)
    pieces, sent = lax.optimization_barrier((pieces, sent))
    halves = [
        lax.all_gather(part, "tok", axis=1, axis_index_groups=rings_x, tiled=True).reshape(
            group * width_here // 2, columns
        )
        for part in jnp.split(pieces, 2)
    ]
    own_weight = jnp.concatenate(halves, axis=0)
    other_halves = [partner(half, "tok", 0) for half in halves]

    gathered = lax.all_to_all(sent, "head", 0, 0, tiled=True)
    rows_here = block_rows // 4
    blocks_shape = pltpu.HBM((RING, width_here, rows_here), jnp.bfloat16)
    tiles = width // LANES
    half_flops = 2 * block_rows * width * columns
    attended, partial, merge_here, early = pl.pallas_call(
        project_kernel,
        out_shape=(
            jax.ShapeDtypeStruct((block_rows, width), jnp.bfloat16),
            jax.ShapeDtypeStruct((tiles, block_rows, LANES), jnp.float32),
            jax.ShapeDtypeStruct(merge_weight.shape, jnp.bfloat16),
            jax.ShapeDtypeStruct(other_halves[1].shape, jnp.bfloat16),
        ),
        in_specs=[VMEM, VMEM, HBM, HBM, HBM],
        out_specs=(VMEM, VMEM, VMEM, VMEM),
        scratch_shapes=[
            pltpu.VMEM((tiles, block_rows, LANES), jnp.float32),
            pltpu.SemaphoreType.DMA((3,)),
        ],
        compiler_params=params,
        cost_estimate=pl.CostEstimate(
            flops=half_flops, bytes_accessed=8 * 2**20, transcendentals=0
        ),
    )(gathered, own_weight, *map(at_hbm, (resid, merge_weight, other_halves[1])))
    projected = pl.pallas_call(
        merge_kernel,
        out_shape=blocks_shape,
        in_specs=[VMEM] * 5,
        out_specs=HBM,
        scratch_shapes=[
            pltpu.VMEM((tiles, block_rows, LANES), jnp.float32),
            pltpu.VMEM((width_here, rows_here), jnp.bfloat16),
            pltpu.SemaphoreType.DMA((RING,)),
        ],
        compiler_params=params,
    )(attended, other_halves[0], early, partial, merge_here)

    image_ids = jnp.arange(owners.shape[0], dtype=jnp.int32)
    place_ids = jnp.arange(places, dtype=jnp.int32)
    image_of = jnp.sum(jnp.where(owners[None, :] == place_ids[:, None], image_ids[None, :], 0), axis=1)
    pair_y = (image_of // 2 % RING).reshape(sides, RING, 2)
    wanted = jnp.sum(
        jnp.where((jnp.arange(RING) == my_y)[None, :, None], pair_y, 0), axis=1
    ).reshape(2 * sides)
    mine = owners == place
    tokens = image_grids[:, 0] * image_grids[:, 1]
    first_token = image_offsets - image_ids // 2 * (2 * block_rows)
    facts = jnp.stack([image_ids // 2 // RING, first_token // 4, tokens // 4])
    facts = jnp.sum(jnp.where(mine[None, :], facts, 0), axis=1)

    blocks = lax.all_to_all(projected, "tok", 0, 0, axis_index_groups=rings_y, tiled=True)
    blocks = pl.pallas_call(
        pick_kernel,
        out_shape=pltpu.HBM((2 * sides, width_here, rows_here), jnp.bfloat16),
        in_specs=[SMEM, ANY],
        out_specs=HBM,
        scratch_shapes=[pltpu.SemaphoreType.DMA((2 * sides,))],
        compiler_params=params,
    )(wanted, blocks)
    blocks = lax.all_to_all(blocks, "tok", 0, 0, axis_index_groups=planes, tiled=True)
    return pl.pallas_call(
        deliver_kernel,
        out_shape=jax.ShapeDtypeStruct((width_here, CAP), jnp.bfloat16),
        in_specs=[SMEM, VMEM],
        out_specs=VMEM,
        compiler_params=params,
    )(facts, blocks).T


def solution(mesh):
    placed = (
        P("tok", None),
        P(),
        P(),
        P(None, "head", None),
        P("head", None),
        P("head", None),
        P("tok"),
        P(),
        P(),
        P(),
    )
    return jax.shard_map(
        on_device, mesh=mesh, in_specs=placed, out_specs=P("tok", "head"), check_vma=False
    )
```
